512 devices in a mesh: seq: 64 (over y, x, core), fsdp: 8 (over z).
Axes of the slice: x: 4, y: 8, z: 8, core: 2. Of those that a mesh axis runs over, the one named last changes fastest.
Arguments:
- activation_entries: bfloat16 [8192, 4096], P('seq', 'fsdp'), may hold values from -6 to 6
- content_mapping_matrix: bfloat16 [4096, 4096], P('seq', 'fsdp'), may hold values from -0.09375 to 0.09375
- content_lagged_blend: float32 [4096], P('fsdp'), may hold values from 0 to 1
- acceptance_vectors: bfloat16 [8192, 4096], P('seq', 'fsdp'), may hold values from -6 to 6
- address_vectors_given: bfloat16 [8192, 4096], P('seq', 'fsdp'), may hold values from -6 to 6
- inline_adaptation_speed: bfloat16 [8192, 4096], P('seq', 'fsdp'), may hold values from 0 to 1
- memory_fading_factors: float32 [8192, 4096], P('seq', 'fsdp'), may hold values from 0.6 to 1
- result_filter_given: bfloat16 [8192, 4096], P('seq', 'fsdp'), may hold values from 0.099609375 to 1.5
- extra_coordinate_factors: float32 [4096], P('fsdp'), may hold values from -0.75 to 0.75
- group_layernorm_scaling: float32 [4096], P('fsdp'), may hold values from 0.1 to 1.9
- group_layernorm_offset: float32 [4096], P('fsdp'), may hold values from -4 to 4
Outputs:
- time_mix: bfloat16 [8192, 4096], P('seq', 'fsdp')
The draws below stay inside these ranges and needn't reach their ends.
All inputs are finite; a program needn't handle non-finite values.
Results may differ from the reference program's by a relative error of at most 0.0056.
Values may be sent and summed in bfloat16 or wider, within the bound.
A program may use at most 64 MiB of HBM per device.

```python
import math
import jax
import jax.numpy as jnp
from jax import lax

EMBED_DIMENSION = 4096
GROUP_TALLY = 64
GROUP_DIMENSION = 64
STEPS_IN_TEXT = 8192


def head_kinds(key):
    share = 0.5
    return jax.random.uniform(jax.random.fold_in(key, 11), (GROUP_TALLY,)) < share


def draw_memory_fading_factors(key, part):
    slow = head_kinds(key)
    address_matrix_lines = jax.random.split(jax.random.fold_in(key, 23), 5)
    total = jnp.exp(jax.random.uniform(address_matrix_lines[0], (GROUP_TALLY,), minval=math.log(0.3), maxval=math.log(1.5)))
    spread = jnp.exp(jax.random.uniform(address_matrix_lines[1], (STEPS_IN_TEXT, GROUP_TALLY, GROUP_DIMENSION), minval=math.log(0.5), maxval=math.log(2.0)))
    quick = jnp.exp(jax.random.uniform(address_matrix_lines[2], (GROUP_TALLY,), minval=math.log(1.0 / 50.0), maxval=math.log(1.0 / 30.0)))
    base = jnp.where(slow, total / STEPS_IN_TEXT, quick)
    adaptation_speeds = base[None, :, None] * spread
    element_series_block = jax.random.randint(address_matrix_lines[3], (STEPS_IN_TEXT, GROUP_TALLY), 0, max(STEPS_IN_TEXT // 8, 1)) == 0
    objective_number = jax.random.uniform(address_matrix_lines[4], (STEPS_IN_TEXT, GROUP_TALLY), minval=0.2, maxval=0.5)
    adaptation_speeds = adaptation_speeds + jnp.where(element_series_block, -jnp.log(1.0 - objective_number), 0.0)[:, :, None]
    return jnp.maximum(jnp.exp(-adaptation_speeds), 0.6).reshape(STEPS_IN_TEXT, EMBED_DIMENSION)


def draw_inline_adaptation_speed(key, part):
    slow = head_kinds(key)
    address_matrix_lines = jax.random.split(jax.random.fold_in(key, 29), 4)
    small = jnp.exp(jax.random.uniform(address_matrix_lines[0], (STEPS_IN_TEXT, GROUP_TALLY, GROUP_DIMENSION), minval=math.log(0.0001), maxval=math.log(0.001)))
    strong = jax.random.uniform(address_matrix_lines[1], (STEPS_IN_TEXT, GROUP_TALLY, GROUP_DIMENSION), minval=0.05, maxval=0.6)
    chosen = jax.random.randint(address_matrix_lines[2], (GROUP_TALLY, GROUP_DIMENSION), 0, 10) < 3
    forced = jax.random.randint(address_matrix_lines[3], (GROUP_TALLY,), 0, GROUP_DIMENSION)
    channel = jnp.arange(GROUP_DIMENSION, dtype=jnp.int32)
    chosen = jnp.logical_or(chosen, channel[None, :] == forced[:, None])
    keep_small = jnp.logical_and(slow[:, None], jnp.logical_not(chosen))
    return jnp.where(keep_small[None, :, :], small, strong).reshape(STEPS_IN_TEXT, EMBED_DIMENSION).astype(jnp.bfloat16)


def block_scale(own_key, shape, shards, least, high):
    level = 1.0
    for dim, shards_of in shards:
        heights = jax.random.uniform(jax.random.fold_in(jax.random.fold_in(own_key, 6), dim), (shards_of,), jnp.float32, least / len(shards), high / len(shards))
        level = level * jnp.repeat(jnp.exp(heights), shape[dim] // shards_of).reshape((-1,) + (1,) * (len(shape) - 1 - dim))
    return level


def normal_values(rng, dims, width, bound, pieces=(), kind=jnp.bfloat16):
    array = jax.random.normal(rng, dims, jnp.float32) * width
    if len(pieces) > 0:
        array = block_scale(rng, dims, pieces, -0.22, 0.18) * array
    return jnp.clip(array, min=-bound, max=bound).astype(kind)


def setup_inputs(seed: int = 0) -> dict:
    seeds = jax.random.split(jax.random.key(seed), 12)
    activation_entries = normal_values(seeds[0], (STEPS_IN_TEXT, EMBED_DIMENSION), 1.0, 6.0, ((0, 64), (1, 8)))
    content_mapping_matrix = normal_values(seeds[1], (EMBED_DIMENSION, EMBED_DIMENSION), EMBED_DIMENSION ** -0.5, 0.09375, ((0, 64), (1, 8)))
    content_lagged_blend = jnp.clip(1.0 * jax.random.uniform(seeds[2], (EMBED_DIMENSION,), jnp.float32) ** block_scale(seeds[2], (EMBED_DIMENSION,), ((0, 8),), -0.2, 0.2), 0.0, 1.0)
    acceptance_vectors = normal_values(seeds[3], (STEPS_IN_TEXT, EMBED_DIMENSION), 1.0, 6.0, ((0, 64), (1, 8)))
    address_vectors_given = normal_values(seeds[4], (STEPS_IN_TEXT, EMBED_DIMENSION), 1.0, 6.0, ((0, 64), (1, 8)))
    inline_adaptation_speed = draw_inline_adaptation_speed(jax.random.fold_in(seeds[11], 71), 0)
    memory_fading_factors = draw_memory_fading_factors(jax.random.fold_in(seeds[11], 71), 0)
    result_filter_given = jnp.clip(0.099609375 + 1.4003906 * jax.random.uniform(seeds[7], (STEPS_IN_TEXT, EMBED_DIMENSION), jnp.float32) ** block_scale(seeds[7], (STEPS_IN_TEXT, EMBED_DIMENSION), ((0, 64), (1, 8)), -0.2, 0.2), 0.099609375, 1.5).astype(jnp.bfloat16)
    extra_coordinate_factors = normal_values(seeds[8], (EMBED_DIMENSION,), 0.05, 0.75, ((0, 8),), jnp.float32)
    group_layernorm_scaling = jnp.clip(1.0 + 0.18 * jax.random.normal(seeds[9], (EMBED_DIMENSION,), jnp.float32), 0.1, 1.9)
    group_layernorm_offset = normal_values(seeds[10], (EMBED_DIMENSION,), 0.3, 4.0, ((0, 8),), jnp.float32)
    return dict(activation_entries=activation_entries, content_mapping_matrix=content_mapping_matrix, content_lagged_blend=content_lagged_blend, acceptance_vectors=acceptance_vectors, address_vectors_given=address_vectors_given, inline_adaptation_speed=inline_adaptation_speed, memory_fading_factors=memory_fading_factors, result_filter_given=result_filter_given, extra_coordinate_factors=extra_coordinate_factors, group_layernorm_scaling=group_layernorm_scaling, group_layernorm_offset=group_layernorm_offset)


norm_eps = 0.00064
unit_eps = 1e-05

def reference(activation_entries, content_mapping_matrix, content_lagged_blend, acceptance_vectors, address_vectors_given, inline_adaptation_speed, memory_fading_factors, result_filter_given, extra_coordinate_factors, group_layernorm_scaling, group_layernorm_offset):
    as_float = activation_entries.astype(jnp.float32)
    shifted = jnp.concatenate([jnp.zeros((1, EMBED_DIMENSION), jnp.float32), as_float[:-1]], axis=0)
    mixed = (as_float + (shifted - as_float) * content_lagged_blend[None, :]).astype(jnp.bfloat16)
    value = jnp.dot(mixed, content_mapping_matrix, preferred_element_type=jnp.float32).astype(jnp.bfloat16)

    def advance(state, inputs):
        rec_row, key_row, rate_row, decay_row, value_row = inputs
        rec_row = rec_row.astype(jnp.float32).reshape(GROUP_TALLY, GROUP_DIMENSION)
        key_row = key_row.astype(jnp.float32).reshape(GROUP_TALLY, GROUP_DIMENSION)
        rate_row = rate_row.astype(jnp.float32).reshape(GROUP_TALLY, GROUP_DIMENSION)
        decay_row = decay_row.reshape(GROUP_TALLY, GROUP_DIMENSION)
        value_row = value_row.astype(jnp.float32).reshape(GROUP_TALLY, GROUP_DIMENSION)
        unit = key_row * lax.rsqrt(lax.optimization_barrier(jnp.sum(key_row * key_row, axis=-1, keepdims=True)) + unit_eps)
        erased = jnp.einsum('hvk,hk->hv', state, -unit, precision=lax.Precision.HIGHEST)
        state = state * decay_row[:, None, :] + erased[:, :, None] * (unit * rate_row)[:, None, :] + value_row[:, :, None] * key_row[:, None, :]
        out_row = jnp.einsum('hvk,hk->hv', state, rec_row, precision=lax.Precision.HIGHEST)
        return (state, out_row)
    initial = jnp.zeros((GROUP_TALLY, GROUP_DIMENSION, GROUP_DIMENSION), jnp.float32)
    final_state, read = lax.scan(advance, initial, (acceptance_vectors, address_vectors_given, inline_adaptation_speed, memory_fading_factors, value))
    centre = read - lax.optimization_barrier(jnp.mean(read, axis=-1, keepdims=True))
    spread = lax.optimization_barrier(jnp.mean(centre * centre, axis=-1, keepdims=True))
    standardized_result = (centre * lax.rsqrt(spread + norm_eps)).reshape(STEPS_IN_TEXT, EMBED_DIMENSION) * group_layernorm_scaling[None, :] + group_layernorm_offset[None, :]
    acceptance_by_group = acceptance_vectors.astype(jnp.float32).reshape(STEPS_IN_TEXT, GROUP_TALLY, GROUP_DIMENSION)
    address_by_group = address_vectors_given.astype(jnp.float32).reshape(STEPS_IN_TEXT, GROUP_TALLY, GROUP_DIMENSION)
    content_by_group = value.astype(jnp.float32).reshape(STEPS_IN_TEXT, GROUP_TALLY, GROUP_DIMENSION)
    scaled_aggregate_figure = lax.optimization_barrier(jnp.sum(acceptance_by_group * address_by_group * extra_coordinate_factors.reshape(GROUP_TALLY, GROUP_DIMENSION)[None], axis=-1, keepdims=True))
    present_extra_term = (scaled_aggregate_figure * content_by_group).reshape(STEPS_IN_TEXT, EMBED_DIMENSION)
    return ((standardized_result + present_extra_term) * result_filter_given.astype(jnp.float32)).astype(jnp.bfloat16)
```

```python
import functools

import jax
import jax.numpy as jnp
from jax import lax
from jax.experimental import pallas as pl
from jax.experimental.pallas import tpu as pltpu
from jax.sharding import PartitionSpec as P

MESH = pl.DeviceIdType.MESH
F32 = jnp.float32
BF16 = jnp.bfloat16
HEAD = 64
HEADS = 8
TOKENS = 128
WIDTH = HEAD * HEADS
NX, NY, NZ = 4, 8, 8
ROW = 2 * NX
NORM_EPS = 0.00064
UNIT_EPS = 1e-05


def split(x):
    high = x.astype(BF16)
    return high, (x - high.astype(F32)).astype(BF16)


def cat(*parts, axis):
    return jnp.concatenate(parts, axis=axis)


def dot(a, b):
    return jnp.dot(a, b, preferred_element_type=F32)


def dot_nt(a, b):
    return lax.dot_general(a, b, (((1,), (1,)), ((), ())), preferred_element_type=F32)


def wide_left(high, low):
    return cat(high, low, high, axis=1)


def wide_right(high, low):
    return cat(high, high, low, axis=0)


def iota(shape, dim):
    return lax.broadcasted_iota(jnp.int32, shape, dim)


def head_sums(x):
    ones = ((iota((256, 256), 0) // HEAD) == (iota((256, 256), 1) // HEAD)).astype(BF16)
    high, low = split(x)
    sums = dot(cat(high[:, :256], high[:, 256:], axis=0), ones) + dot(
        cat(low[:, :256], low[:, 256:], axis=0), ones
    )
    return cat(sums[:TOKENS], sums[TOKENS:], axis=1)


def shift_rows(x, steps, fill):
    rows = iota(x.shape, 0)
    return jnp.where(rows < steps, fill, pltpu.roll(x, steps, 0))


def prepare(r_ref, k_ref, a_ref, w_ref, bonus_ref, y_ref, q_ref, h_ref, g_ref, coef_ref):
    r = r_ref[...].astype(F32)
    k = k_ref[...].astype(F32)
    a = a_ref[...].astype(F32)
    unit = k * lax.rsqrt(head_sums(k * k) + UNIT_EPS)
    coef_ref[...] = head_sums(r * k * bonus_ref[...])
    cumul = w_ref[...]
    for level in range(7):
        cumul = cumul * shift_rows(cumul, 1 << level, 1.0)
    before = shift_rows(cumul, 1, 1.0)
    inverse = 1.0 / cumul
    end = cumul[TOKENS - 1 :, :]
    erase = -unit * before
    write = unit * a * inverse
    key = k * inverse
    rec = r * cumul
    erase_h, erase_l = split(erase)
    write_h, write_l = split(write)
    key_h, key_l = split(key)
    rec_h, rec_l = split(rec)
    write_end = write * end
    key_end = key * end
    rows, cols = iota((TOKENS, TOKENS), 0), iota((TOKENS, TOKENS), 1)
    strict, inclusive = rows > cols, rows >= cols
    differ = rows ^ cols
    eye = (rows == cols).astype(F32)
    small_eye = iota((HEAD, HEAD), 0) == iota((HEAD, HEAD), 1)

    grams, solves = [], []
    for h in range(HEADS):
        at = slice(HEAD * h, HEAD * (h + 1))
        left = wide_left(
            cat(erase_h[:, at], rec_h[:, at], axis=0), cat(erase_l[:, at], rec_l[:, at], axis=0)
        )
        right = wide_left(
            cat(write_h[:, at], key_h[:, at], axis=0), cat(write_l[:, at], key_l[:, at], axis=0)
        )
        right = cat(right[:, :HEAD], right[:, :HEAD], right[:, HEAD : 2 * HEAD], axis=1)
        grams.append(dot_nt(left, right))
    systems = [jnp.where(strict, gram[:TOKENS, :TOKENS], 0.0) for gram in grams]
    halves = [split(system) for system in systems]
    for h in range(HEADS):
        solves.append(eye + jnp.where(differ == 1, systems[h], 0.0))
    for level in range(1, 7):
        mask = (differ >> level) == 1
        for h in range(HEADS):
            rough = solves[h].astype(BF16)
            part = jnp.where(mask, halves[h][0], jnp.zeros_like(halves[h][0]))
            solves[h] = solves[h] + dot(rough, dot(part, rough).astype(BF16))
    for h in range(HEADS):
        high, low = split(solves[h])
        left_over = eye - solves[h] + dot(wide_left(*halves[h]), wide_right(high, low))
        solves[h] = solves[h] + dot(high, left_over.astype(BF16))
    for pair in range(HEADS // 2):
        wide = slice(2 * HEAD * pair, 2 * HEAD * (pair + 1))
        write_t = write_end[:, wide].T
        key_t = key_end[:, wide].T
        for half in range(2):
            h = 2 * pair + half
            at = slice(HEAD * h, HEAD * (h + 1))
            gram = grams[h]
            erase_key = split(jnp.where(strict, gram[:TOKENS, TOKENS:], 0.0))
            read_write = jnp.where(inclusive, gram[TOKENS:, :TOKENS], 0.0)
            read_key = jnp.where(inclusive, gram[TOKENS:, TOKENS:], 0.0)
            both = dot(
                wide_left(*split(solves[h])),
                wide_right(
                    cat(erase_key[0], erase_h[:, at], axis=1),
                    cat(erase_key[1], erase_l[:, at], axis=1),
                ),
            )
            mine = slice(HEAD * half, HEAD * (half + 1))
            out = dot(
                wide_left(*split(cat(read_write, write_t[mine], axis=0))),
                wide_right(*split(both)),
            )
            y_ref[h] = cat(*split(read_key + out[:TOKENS, :TOKENS]), axis=1)
            q_ref[h] = cat(*split(rec[:, at] + out[:TOKENS, TOKENS:]), axis=1)
            h_ref[h] = cat(*split(key_t[mine] + out[TOKENS:, :TOKENS]), axis=1)
            diagonal = jnp.where(small_eye, end[:, at], 0.0)
            g_ref[h] = cat(*split(diagonal + out[TOKENS:, TOKENS:]), axis=1)


PREPARED = (
    ((HEADS, TOKENS, 2 * TOKENS), BF16),
    ((HEADS, TOKENS, 2 * HEAD), BF16),
    ((HEADS, HEAD, 2 * TOKENS), BF16),
    ((HEADS, HEAD, 2 * HEAD), BF16),
    ((TOKENS, WIDTH), F32),
)


def chain_step(g, z):
    high, low = split(z)
    return dot(cat(g, g[:, :HEAD], axis=1), wide_right(high, low))


def fold(x):
    return x[:, :HEAD] + x[:, HEAD:]


def pack(x):
    return cat(*split(x), axis=1)


def exchange(
    x_ref, w_ref, blend_ref, y_ref, q_ref, h_ref, g_ref, coef_ref, gate_ref, scale_ref, offset_ref,
    out_ref,
    prev_buf, x_send, xg, wa, wb, p_send, p_recv,
    g_row, g_col, z_chain, z_all, z_row,
    l_send, l_row, t_send, t_col, s_send, s_in,
    send, recv, local,
):
    s, z = lax.axis_index("seq"), lax.axis_index("fsdp")
    count = NX * NY * 2
    core, x, y, place = s % 2, (s // 2) % NX, s // ROW, s % ROW
    counter = iter(range(10**6))
    waiting, conditional = [], []

    def at_seq(index):
        return {"seq": index}

    def chip(yy, xx):
        return at_seq((yy * NX + xx) * 2 + core)

    def copy_to(source, target, device):
        n = next(counter)
        copy = pltpu.make_async_remote_copy(
            src_ref=source, dst_ref=target, send_sem=send.at[n], recv_sem=recv.at[n],
            device_id=device, device_id_type=MESH,
        )
        copy.start()
        entry = [copy, False]
        waiting.append(entry)
        return entry

    def arrived(entry):
        if not entry[1]:
            entry[1] = True
            entry[0].wait_recv()

    own_a = pltpu.make_async_copy(w_ref.at[:, pl.ds(0, 256)], wa.at[y, x], local.at[0])
    own_b = pltpu.make_async_copy(w_ref.at[:, pl.ds(256, 256)], wb.at[y, x], local.at[1])
    own_a.start()
    own_b.start()
    for d in range(NY):
        t_col[d] = jnp.zeros((HEAD, 2 * HEAD), BF16)
    barrier = pltpu.get_barrier_semaphore()
    partners = [at_seq(y * ROW + (place + d) % ROW) for d in range(1, ROW)]
    partners += [chip((y + d) % NY, x) for d in range(1, NY)]
    partners += [{"fsdp": (z + 1) % NZ}, {"fsdp": (z + NZ - 1) % NZ}]
    partners += [at_seq((s + 1) % count), at_seq((s + count - 1) % count)]
    for partner in partners:
        pl.semaphore_signal(barrier, inc=1, device_id=partner, device_id_type=MESH)
    pl.semaphore_wait(barrier, len(partners))
    own_a.wait()
    own_b.wait()

    right, left = (x + 1) % NX, (x + NX - 1) % NX
    sides = (1, -1)

    prev = copy_to(x_ref.at[pl.ds(TOKENS - 16, 16)], prev_buf, at_seq((s + 1) % count))
    a_in = [copy_to(wa.at[y, x], wa.at[y, x], chip(y, (x + d) % NX)) for d in range(1, NX)]

    yb = {}
    xb = {}

    def row_at(offset):
        return (y + offset + NY) % NY

    def send_yb(step):
        for side in sides:
            if step > 1:
                arrived(yb[side, step - 1])
            if step == NY // 2 and side < 0:
                continue
            row = row_at(-side * (step - 1))
            yb[side, step] = copy_to(wb.at[row, x], wb.at[row, x], chip(row_at(side), x))

    def send_xb(offset):
        row = row_at(offset)
        for side, to in ((1, right), (-1, left)):
            xb[side, offset] = copy_to(wb.at[row, x], wb.at[row, x], chip(y, to))

    def forward_xb(offset):
        row = row_at(offset)
        if offset % 2 == 0:
            arrived(xb[1, offset])
            copy_to(wb.at[row, left], wb.at[row, left], chip(y, right))
        else:
            arrived(xb[-1, offset])
            copy_to(wb.at[row, right], wb.at[row, right], chip(y, left))

    send_yb(1)
    send_xb(0)

    arrived(prev)
    own = x_ref[...].astype(F32)
    before = jnp.where(s == 0, 0.0, prev_buf[...].astype(F32)[15:16, :])
    shifted = jnp.where(iota((TOKENS, WIDTH), 0) == 0, before, pltpu.roll(own, 1, 0))
    mixed = own + (shifted - own) * blend_ref[...]
    even = cat(*[mixed[:, 128 * q : 128 * q + 64] for q in range(4)], axis=1).astype(BF16)
    odd = cat(*[mixed[:, 128 * q + 64 : 128 * q + 128] for q in range(4)], axis=1).astype(BF16)
    is_even = core == 0
    xg[z, core] = jnp.where(is_even, even, odd)
    x_send[...] = jnp.where(is_even, odd, even)
    mate = at_seq(s + 1 - 2 * core)
    mate_x = copy_to(x_send, xg.at[z, core], mate)

    zx, ya = {}, {}

    def send_zx(step, sub):
        part = core if sub == 0 else 1 - core
        for side in sides:
            if step == NZ // 2 and side != sides[sub]:
                continue
            if step > 1:
                arrived(zx[side, step - 1, sub])
            block = (z + NZ - side * (step - 1)) % NZ
            zx[side, step, sub] = copy_to(
                xg.at[block, part], xg.at[block, part], {"fsdp": (z + NZ + side) % NZ}
            )

    def send_ya(step, sub):
        for side in sides:
            if step == NY // 2 and side != sides[sub]:
                continue
            if step > 1:
                arrived(ya[side, step - 1, sub])
            row = row_at(-side * (step - 1))
            part = wa.at[row, pl.ds(2 * sub, 2)]
            ya[side, step, sub] = copy_to(part, part, chip(row_at(side), x))

    send_zx(1, 0)
    for entry in a_in:
        arrived(entry)
    send_ya(1, 0)
    send_ya(1, 1)
    arrived(mate_x)
    send_zx(1, 1)

    g_in = []
    g_row[place] = g_ref[place]
    for d in range(1, ROW):
        to = (place + d) % ROW
        g_in.append(copy_to(g_ref.at[to], g_row.at[place], at_seq(y * ROW + to)))

    def round_of(step):
        for sub in range(2):
            send_ya(step, sub)
            send_zx(step, sub)
            if sub == 0:
                send_yb(step)
                for offset in (-(step - 1), step - 1):
                    send_xb(offset)
            else:
                if step == 2:
                    forward_xb(0)
                else:
                    for offset in (-(step - 2), step - 2):
                        forward_xb(offset)

    def row_chain():
        for entry in g_in:
            arrived(entry)
        wide = z_chain.shape[1]
        lane, line = iota((HEAD, wide), 1), iota((HEAD, wide), 0)
        chain = (lane == line + ROW * HEAD).astype(F32)
        for j in range(ROW):
            z_all[j] = cat(*split(chain), axis=1)
            chain = chain_step(g_row[j], chain) + (lane == line + j * HEAD).astype(F32)
        z_chain[...] = chain

    def send_g_col():
        total = pack(z_chain[...][:, ROW * HEAD : (ROW + 1) * HEAD])
        g_col[y] = total
        for d in range(1, NY):
            n = next(counter)
            conditional.append(
                (d, n, pltpu.make_async_remote_copy(
                    src_ref=g_col.at[y], dst_ref=g_col.at[y], send_sem=send.at[n], recv_sem=recv.at[n],
                    device_id=chip((y + d) % NY, x), device_id_type=MESH,
                ))
            )

            @pl.when(y + d < NY)
            def _(copy=conditional[-1][2]):
                copy.start()

    def column_chain():
        for d, _, copy in conditional[: NY - 1]:

            @pl.when(y >= d)
            def _(copy=copy):
                copy.wait_recv()

        lane, line = iota((HEAD, NY * HEAD), 1), iota((HEAD, NY * HEAD), 0)
        chain = jnp.zeros((HEAD, NY * HEAD), F32)
        for q in range(NY - 1):
            longer = chain_step(g_col[q], chain) + (lane == line + q * HEAD).astype(F32)
            chain = jnp.where(q < y, longer, chain)
        z_row[...] = cat(*split(chain), axis=0)

    round_of(2)
    row_chain()
    round_of(3)
    send_g_col()
    round_of(4)
    column_chain()
    arrived(yb[1, NY // 2])
    send_xb(-4)
    forward_xb(-3)
    forward_xb(3)
    forward_xb(-4)
    for entry in waiting:
        arrived(entry)

    parts = {}
    for mine in (False, True):
        block = core if mine else 1 - core
        for half, weights in enumerate((wa, wb)):
            total = jnp.zeros((TOKENS, 256), F32)
            for row in range(NY):
                total = total + dot(xg[row, block], weights[row].reshape(256, 256))
            if mine:
                parts[half] = total
            else:
                p_send[half] = total
                parts[half, "copy"] = copy_to(p_send.at[half], p_recv.at[half], mate)
    values = []
    for half in range(2):
        arrived(parts[half, "copy"])
        values.append((parts[half] + p_recv[half]).astype(BF16))
    value = cat(*values, axis=1)

    doubled = []
    for h in range(HEADS):
        v = value[:, HEAD * h : HEAD * (h + 1)]
        doubled.append(cat(v, v, axis=0))
        l_send[h] = pack(dot(h_ref[h], doubled[h]))
    l_in = []
    for d in range(1, ROW):
        to = (place + d) % ROW
        l_in.append(copy_to(l_send.at[to], l_row.at[place], at_seq(y * ROW + to)))
    l_row[place] = l_send[place]
    chain = z_chain[...][:, : ROW * HEAD]
    row_total = cat(*split(chain), axis=0)
    for entry in l_in:
        arrived(entry)
    lows = l_row[...].reshape(ROW * HEAD, 2 * HEAD)
    total = fold(dot(row_total, lows))
    t_send[...] = pack(total[:HEAD] + total[HEAD:])
    first = len(conditional)
    for d in range(1, NY):
        n = next(counter)
        conditional.append(
            (d, n, pltpu.make_async_remote_copy(
                src_ref=t_send, dst_ref=t_col.at[y], send_sem=send.at[n], recv_sem=recv.at[n],
                device_id=chip((y + d) % NY, x), device_id_type=MESH,
            ))
        )

        @pl.when(y + d < NY)
        def _(copy=conditional[-1][2]):
            copy.start()

    wide = ROW * HEAD
    span = z_all.shape[2] // 2
    from_row = []
    for j in range(ROW):
        both = cat(z_all[j, :, :wide], z_all[j, :, span : span + wide], axis=1)
        from_row.append(dot(both, cat(lows, lows, axis=0)))
    reads = [dot(y_ref[h], doubled[h]) for h in range(HEADS)]
    extra = coef_ref[...] * value.astype(F32)
    gate = gate_ref[...].astype(F32)

    for d, _, copy in conditional[first:]:

        @pl.when(y >= d)
        def _(copy=copy):
            copy.wait_recv()

    entering = fold(dot(z_row[...], t_col[...].reshape(NY * HEAD, 2 * HEAD)))
    entering = pack(entering[:HEAD] + entering[HEAD:])
    twice = cat(entering, entering, axis=0)
    for j in range(ROW):
        both = cat(
            z_all[j, :, wide : wide + HEAD], z_all[j, :, span + wide : span + wide + HEAD], axis=1
        )
        s_send[j] = pack(fold(from_row[j] + dot(both, twice)))
    s_wait = []
    for d in range(1, ROW):
        to = (place + d) % ROW
        s_wait.append(copy_to(s_send.at[to], s_in.at[place], at_seq(y * ROW + to)))
    s_in[place] = s_send[place]
    for entry in s_wait:
        arrived(entry)
    for h in range(HEADS):
        state = s_in[h]
        reads[h] = reads[h] + fold(dot(q_ref[h], cat(state, state, axis=0)))
    read = cat(*reads, axis=1)
    centre = read - head_sums(read) * (1.0 / HEAD)
    spread = head_sums(centre * centre) * (1.0 / HEAD)
    normed = centre * lax.rsqrt(spread + NORM_EPS) * scale_ref[...] + offset_ref[...]
    out_ref[...] = ((normed + extra) * gate).astype(BF16)

    for entry in waiting:
        entry[0].wait_send()
    for d, _, copy in conditional:

        @pl.when(y + d < NY)
        def _(copy=copy):
            copy.wait_send()


COPIES = 128
SCRATCH = (
    pltpu.VMEM((16, WIDTH), BF16),
    pltpu.VMEM((TOKENS, 256), BF16),
    pltpu.VMEM((NZ, 2, TOKENS, 256), BF16),
    pltpu.VMEM((NY, NX, HEAD, 256), BF16),
    pltpu.VMEM((NY, NX, HEAD, 256), BF16),
    pltpu.VMEM((2, TOKENS, 256), F32),
    pltpu.VMEM((2, TOKENS, 256), F32),
    pltpu.VMEM((ROW, HEAD, 2 * HEAD), BF16),
    pltpu.VMEM((NY, HEAD, 2 * HEAD), BF16),
    pltpu.VMEM((HEAD, 640), F32),
    pltpu.VMEM((ROW, HEAD, 2 * 640), BF16),
    pltpu.VMEM((2 * HEAD, NY * HEAD), BF16),
    pltpu.VMEM((HEADS, HEAD, 2 * HEAD), BF16),
    pltpu.VMEM((ROW, HEAD, 2 * HEAD), BF16),
    pltpu.VMEM((HEAD, 2 * HEAD), BF16),
    pltpu.VMEM((NY, HEAD, 2 * HEAD), BF16),
    pltpu.VMEM((ROW, HEAD, 2 * HEAD), BF16),
    pltpu.VMEM((HEADS, HEAD, 2 * HEAD), BF16),
    pltpu.SemaphoreType.DMA((COPIES,)),
    pltpu.SemaphoreType.DMA((COPIES,)),
    pltpu.SemaphoreType.DMA((2,)),
)


def shards(
    activation_entries,
    content_mapping_matrix,
    content_lagged_blend,
    acceptance_vectors,
    address_vectors_given,
    inline_adaptation_speed,
    memory_fading_factors,
    result_filter_given,
    extra_coordinate_factors,
    group_layernorm_scaling,
    group_layernorm_offset,
):
    vmem = pl.BlockSpec(memory_space=pltpu.VMEM)

    def row(vector):
        return vector.reshape(1, WIDTH)

    prepared = pl.pallas_call(
        prepare,
        out_shape=[jax.ShapeDtypeStruct(shape, kind) for shape, kind in PREPARED],
        in_specs=[vmem] * 5,
        out_specs=[vmem] * len(PREPARED),
        compiler_params=pltpu.CompilerParams(vmem_limit_bytes=56 << 20),
        name="prepare",
    )(
        acceptance_vectors,
        address_vectors_given,
        inline_adaptation_speed,
        memory_fading_factors,
        row(extra_coordinate_factors),
    )
    return pl.pallas_call(
        exchange,
        out_shape=jax.ShapeDtypeStruct((TOKENS, WIDTH), BF16),
        in_specs=[vmem] * 11,
        out_specs=vmem,
        scratch_shapes=SCRATCH,
        compiler_params=pltpu.CompilerParams(
            collective_id=0, has_side_effects=True, vmem_limit_bytes=56 << 20
        ),
        name="exchange",
    )(
        activation_entries,
        content_mapping_matrix,
        row(content_lagged_blend),
        *prepared,
        result_filter_given,
        row(group_layernorm_scaling),
        row(group_layernorm_offset),
    )


def solution(mesh):
    return jax.shard_map(
        shards,
        mesh=mesh,
        in_specs=(
            P("seq", "fsdp"),
            P("seq", "fsdp"),
            P("fsdp"),
            P("seq", "fsdp"),
            P("seq", "fsdp"),
            P("seq", "fsdp"),
            P("seq", "fsdp"),
            P("seq", "fsdp"),
            P("fsdp"),
            P("fsdp"),
            P("fsdp"),
        ),
        out_specs=P("seq", "fsdp"),
        check_vma=False,
    )
```

```python
import functools

import jax
import jax.numpy as jnp
from jax import lax
from jax.experimental import pallas as pl
from jax.experimental.pallas import tpu as pltpu
from jax.sharding import PartitionSpec as P

MESH = pl.DeviceIdType.MESH
F32 = jnp.float32
BF16 = jnp.bfloat16
HEAD = 64
HEADS = 8
TOKENS = 128
WIDTH = HEAD * HEADS
NX, NY, NZ = 4, 8, 8
ROW = 2 * NX
NORM_EPS = 0.00064
UNIT_EPS = 1e-05


def split(x):
    high = x.astype(BF16)
    return high, (x - high.astype(F32)).astype(BF16)


def cat(*parts, axis):
    return jnp.concatenate(parts, axis=axis)


def dot(a, b):
    return jnp.dot(a, b, preferred_element_type=F32)


def dot_nt(a, b):
    return lax.dot_general(a, b, (((1,), (1,)), ((), ())), preferred_element_type=F32)


def wide_left(high, low):
    return cat(high, low, high, axis=1)


def wide_right(high, low):
    return cat(high, high, low, axis=0)


def iota(shape, dim):
    return lax.broadcasted_iota(jnp.int32, shape, dim)


def head_sums(x):
    ones = ((iota((256, 256), 0) // HEAD) == (iota((256, 256), 1) // HEAD)).astype(BF16)
    high, low = split(x)
    sums = dot(cat(high[:, :256], high[:, 256:], axis=0), ones) + dot(
        cat(low[:, :256], low[:, 256:], axis=0), ones
    )
    return cat(sums[:TOKENS], sums[TOKENS:], axis=1)


def shift_rows(x, steps, fill):
    rows = iota(x.shape, 0)
    return jnp.where(rows < steps, fill, pltpu.roll(x, steps, 0))


def prepare(r_ref, k_ref, a_ref, w_ref, bonus_ref, y_ref, q_ref, h_ref, g_ref, coef_ref):
    r = r_ref[...].astype(F32)
    k = k_ref[...].astype(F32)
    a = a_ref[...].astype(F32)
    unit = k * lax.rsqrt(head_sums(k * k) + UNIT_EPS)
    coef_ref[...] = head_sums(r * k * bonus_ref[...])
    cumul = w_ref[...]
    for level in range(7):
        cumul = cumul * shift_rows(cumul, 1 << level, 1.0)
    yield
    before = shift_rows(cumul, 1, 1.0)
    inverse = 1.0 / cumul
    end = cumul[TOKENS - 1 :, :]
    erase = -unit * before
    write = unit * a * inverse
    key = k * inverse
    rec = r * cumul
    erase_h, erase_l = split(erase)
    write_h, write_l = split(write)
    key_h, key_l = split(key)
    rec_h, rec_l = split(rec)
    write_end = write * end
    key_end = key * end
    rows, cols = iota((TOKENS, TOKENS), 0), iota((TOKENS, TOKENS), 1)
    strict, inclusive = rows > cols, rows >= cols
    differ = rows ^ cols
    eye = (rows == cols).astype(F32)
    small_eye = iota((HEAD, HEAD), 0) == iota((HEAD, HEAD), 1)

    grams, solves = [], []
    for h in range(HEADS):
        at = slice(HEAD * h, HEAD * (h + 1))
        left = wide_left(
            cat(erase_h[:, at], rec_h[:, at], axis=0), cat(erase_l[:, at], rec_l[:, at], axis=0)
        )
        high = cat(write_h[:, at], key_h[:, at], axis=0)
        low = cat(write_l[:, at], key_l[:, at], axis=0)
        grams.append(dot_nt(left, cat(high, high, low, axis=1)))
        if h == HEADS // 2 - 1:
            yield
    systems = [jnp.where(strict, gram[:TOKENS, :TOKENS], 0.0) for gram in grams]
    halves = [split(system) for system in systems]
    for h in range(HEADS):
        solves.append(eye + jnp.where(differ == 1, systems[h], 0.0))
    yield
    for level in range(1, 7):
        mask = (differ >> level) == 1
        for h in range(HEADS):
            rough = solves[h].astype(BF16)
            part = jnp.where(mask, halves[h][0], jnp.zeros_like(halves[h][0]))
            solves[h] = solves[h] + dot(rough, dot(part, rough).astype(BF16))
        yield
    for h in range(HEADS):
        high, low = split(solves[h])
        left_over = eye - solves[h] + dot(wide_left(*halves[h]), wide_right(high, low))
        solves[h] = solves[h] + dot(high, left_over.astype(BF16))
    yield
    for pair in range(HEADS // 2):
        wide = slice(2 * HEAD * pair, 2 * HEAD * (pair + 1))
        write_t = write_end[:, wide].T
        key_t = key_end[:, wide].T
        for half in range(2):
            h = 2 * pair + half
            at = slice(HEAD * h, HEAD * (h + 1))
            gram = grams[h]
            erase_key = split(jnp.where(strict, gram[:TOKENS, TOKENS:], 0.0))
            read_write = jnp.where(inclusive, gram[TOKENS:, :TOKENS], 0.0)
            read_key = jnp.where(inclusive, gram[TOKENS:, TOKENS:], 0.0)
            both = dot(
                wide_left(*split(solves[h])),
                wide_right(
                    cat(erase_key[0], erase_h[:, at], axis=1),
                    cat(erase_key[1], erase_l[:, at], axis=1),
                ),
            )
            mine = slice(HEAD * half, HEAD * (half + 1))
            out = dot(
                wide_left(*split(cat(read_write, write_t[mine], axis=0))),
                wide_right(*split(both)),
            )
            y_ref[h] = cat(*split(read_key + out[:TOKENS, :TOKENS]), axis=1)
            q_ref[h] = cat(*split(rec[:, at] + out[:TOKENS, TOKENS:]), axis=1)
            h_ref[h] = cat(*split(key_t[mine] + out[TOKENS:, :TOKENS]), axis=1)
            diagonal = jnp.where(small_eye, end[:, at], 0.0)
            g_ref[h] = cat(*split(diagonal + out[TOKENS:, TOKENS:]), axis=1)
        yield


def chain_step(g, z):
    high, low = split(z)
    return dot(cat(g, g[:, :HEAD], axis=1), wide_right(high, low))


def fold(x):
    return x[:, :HEAD] + x[:, HEAD:]


def pack(x):
    return cat(*split(x), axis=1)


def time_mix(
    x_hbm, w_ref, r_hbm, k_hbm, a_hbm, decay_hbm, gate_hbm, blend_ref, bonus_ref, scale_ref, offset_ref,
    out_ref,
    x_ref, r_ref, k_ref, a_ref, decay_ref, gate_ref,
    y_ref, q_ref, h_ref, g_ref, coef_ref,
    prev_buf, x_send, xg, wa, wb, p_send, p_recv,
    g_row, g_col, z_chain, z_all, z_row,
    l_send, l_row, t_send, t_col, s_send, s_in,
    send, recv, local,
):
    s, z = lax.axis_index("seq"), lax.axis_index("fsdp")
    count = NX * NY * 2
    core, x, y, place = s % 2, (s // 2) % NX, s // ROW, s % ROW
    counter = iter(range(10**6))
    waiting, conditional = [], []

    def at_seq(index):
        return {"seq": index}

    def chip(yy, xx):
        return at_seq((yy * NX + xx) * 2 + core)

    def copy_to(source, target, device):
        n = next(counter)
        copy = pltpu.make_async_remote_copy(
            src_ref=source, dst_ref=target, send_sem=send.at[n], recv_sem=recv.at[n],
            device_id=device, device_id_type=MESH,
        )
        copy.start()
        entry = [copy, False]
        waiting.append(entry)
        return entry

    def arrived(entry):
        if not entry[1]:
            entry[1] = True
            entry[0].wait_recv()

    def finish():
        for entry in waiting:
            entry[0].wait_send()
        for d, _, copy in conditional:

            @pl.when(y + d < NY)
            def _(copy=copy):
                copy.wait_send()

    loads = [
        pltpu.make_async_copy(source, target, local.at[n])
        for n, (source, target) in enumerate(
            (
                (w_ref.at[:, pl.ds(0, 256)], wa.at[y, x]),
                (w_ref.at[:, pl.ds(256, 256)], wb.at[y, x]),
                (x_hbm, x_ref),
                (r_hbm, r_ref),
                (k_hbm, k_ref),
                (a_hbm, a_ref),
                (decay_hbm, decay_ref),
                (gate_hbm, gate_ref),
            )
        )
    ]
    for load in loads:
        load.start()
    for d in range(NY):
        t_col[d] = jnp.zeros((HEAD, 2 * HEAD), BF16)
    barrier = pltpu.get_barrier_semaphore()
    partners = [at_seq(y * ROW + (place + d) % ROW) for d in range(1, ROW)]
    partners += [chip((y + d) % NY, x) for d in range(1, NY)]
    partners += [{"fsdp": (z + 1) % NZ}, {"fsdp": (z + NZ - 1) % NZ}]
    partners += [at_seq((s + 1) % count), at_seq((s + count - 1) % count)]
    for partner in partners:
        pl.semaphore_signal(barrier, inc=1, device_id=partner, device_id_type=MESH)
    pl.semaphore_wait(barrier, len(partners))
    for load in loads:
        load.wait()

    right, left = (x + 1) % NX, (x + NX - 1) % NX
    sides = (1, -1)

    a_in = [copy_to(wa.at[y, x], wa.at[y, x], chip(y, (x + d) % NX)) for d in range(1, NX)]
    prev = copy_to(x_ref.at[pl.ds(TOKENS - 16, 16)], prev_buf, at_seq((s + 1) % count))

    yb = {}
    xb = {}

    def row_at(offset):
        return (y + offset + NY) % NY

    def send_yb(step):
        for side in sides:
            if step > 1:
                arrived(yb[side, step - 1])
            if step == NY // 2 and side < 0:
                continue
            row = row_at(-side * (step - 1))
            yb[side, step] = copy_to(wb.at[row, x], wb.at[row, x], chip(row_at(side), x))

    def send_xb(offset):
        row = row_at(offset)
        for side, to in ((1, right), (-1, left)):
            xb[side, offset] = copy_to(wb.at[row, x], wb.at[row, x], chip(y, to))

    def forward_xb(offset):
        row = row_at(offset)
        if offset % 2 == 0:
            arrived(xb[1, offset])
            copy_to(wb.at[row, left], wb.at[row, left], chip(y, right))
        else:
            arrived(xb[-1, offset])
            copy_to(wb.at[row, right], wb.at[row, right], chip(y, left))

    zx, ya = {}, {}

    def send_zx(step, sub):
        part = core if sub == 0 else 1 - core
        for side in sides:
            if step == NZ // 2 and side != sides[sub]:
                continue
            if step > 1:
                arrived(zx[side, step - 1, sub])
            block = (z + NZ - side * (step - 1)) % NZ
            zx[side, step, sub] = copy_to(
                xg.at[block, part], xg.at[block, part], {"fsdp": (z + NZ + side) % NZ}
            )

    def send_ya(step, sub):
        for side in sides:
            if step == NY // 2 and side != sides[sub]:
                continue
            if step > 1:
                arrived(ya[side, step - 1, sub])
            row = row_at(-side * (step - 1))
            part = wa.at[row, pl.ds(2 * sub, 2)]
            ya[side, step, sub] = copy_to(part, part, chip(row_at(side), x))

    def row_chain():
        for entry in g_in:
            arrived(entry)
        wide = z_chain.shape[1]
        lane, line = iota((HEAD, wide), 1), iota((HEAD, wide), 0)
        chain = (lane == line + ROW * HEAD).astype(F32)
        for j in range(ROW):
            z_all[j] = cat(*split(chain), axis=1)
            chain = chain_step(g_row[j], chain) + (lane == line + j * HEAD).astype(F32)
        z_chain[...] = chain

    def send_g_col():
        total = pack(z_chain[...][:, ROW * HEAD : (ROW + 1) * HEAD])
        g_col[y] = total
        for d in range(1, NY):
            n = next(counter)
            conditional.append(
                (d, n, pltpu.make_async_remote_copy(
                    src_ref=g_col.at[y], dst_ref=g_col.at[y], send_sem=send.at[n], recv_sem=recv.at[n],
                    device_id=chip((y + d) % NY, x), device_id_type=MESH,
                ))
            )

            @pl.when(y + d < NY)
            def _(copy=conditional[-1][2]):
                copy.start()

    def column_chain():
        for d, _, copy in conditional[: NY - 1]:

            @pl.when(y >= d)
            def _(copy=copy):
                copy.wait_recv()

        lane, line = iota((HEAD, NY * HEAD), 1), iota((HEAD, NY * HEAD), 0)
        chain = jnp.zeros((HEAD, NY * HEAD), F32)
        for q in range(NY - 1):
            longer = chain_step(g_col[q], chain) + (lane == line + q * HEAD).astype(F32)
            chain = jnp.where(q < y, longer, chain)
        z_row[...] = cat(*split(chain), axis=0)

    stages = prepare(
        r_ref, k_ref, a_ref, decay_ref, bonus_ref, y_ref, q_ref, h_ref, g_ref, coef_ref
    )

    def compute(steps=1):
        for _ in range(steps):
            next(stages, None)

    send_yb(1)
    send_xb(0)
    compute()
    for entry in a_in:
        arrived(entry)
    send_ya(1, 0)
    send_ya(1, 1)

    arrived(prev)
    own = x_ref[...].astype(F32)
    before = jnp.where(s == 0, 0.0, prev_buf[...].astype(F32)[15:16, :])
    shifted = jnp.where(iota((TOKENS, WIDTH), 0) == 0, before, pltpu.roll(own, 1, 0))
    mixed = own + (shifted - own) * blend_ref[...]
    even = cat(*[mixed[:, 128 * q : 128 * q + 64] for q in range(4)], axis=1).astype(BF16)
    odd = cat(*[mixed[:, 128 * q + 64 : 128 * q + 128] for q in range(4)], axis=1).astype(BF16)
    is_even = core == 0
    xg[z, core] = jnp.where(is_even, even, odd)
    x_send[...] = jnp.where(is_even, odd, even)
    mate = at_seq(s + 1 - 2 * core)
    mate_x = copy_to(x_send, xg.at[z, core], mate)

    send_zx(1, 0)
    send_yb(2)
    send_xb(-1)
    send_xb(1)
    forward_xb(0)
    arrived(mate_x)
    send_zx(1, 1)
    compute()
    send_ya(2, 0)
    send_zx(2, 0)
    send_yb(3)
    send_xb(-2)
    send_xb(2)
    forward_xb(-1)
    forward_xb(1)
    compute(2)
    send_ya(2, 1)
    send_zx(2, 1)
    send_yb(4)
    send_xb(-3)
    send_xb(3)
    forward_xb(-2)
    forward_xb(2)
    compute(2)
    send_ya(3, 0)
    send_zx(3, 0)
    arrived(yb[1, NY // 2])
    send_xb(-4)
    forward_xb(-3)
    forward_xb(3)
    compute(2)
    send_ya(3, 1)
    send_zx(3, 1)
    forward_xb(-4)
    compute(3)
    send_ya(4, 0)
    send_zx(4, 0)
    compute(2)
    send_ya(4, 1)
    send_zx(4, 1)
    compute(100)

    g_in = []
    g_row[place] = g_ref[place]
    for d in range(1, ROW):
        to = (place + d) % ROW
        g_in.append(copy_to(g_ref.at[to], g_row.at[place], at_seq(y * ROW + to)))
    row_chain()
    send_g_col()
    for entry in waiting:
        arrived(entry)

    parts = {}
    for mine in (False, True):
        block = core if mine else 1 - core
        for half, weights in enumerate((wa, wb)):
            total = jnp.zeros((TOKENS, 256), F32)
            for row in range(NY):
                total = total + dot(xg[row, block], weights[row].reshape(256, 256))
            if mine:
                parts[half] = total
            else:
                p_send[half] = total
                parts[half, "copy"] = copy_to(p_send.at[half], p_recv.at[half], mate)
    values = []
    for half in range(2):
        arrived(parts[half, "copy"])
        values.append((parts[half] + p_recv[half]).astype(BF16))
    value = cat(*values, axis=1)

    doubled = []
    for h in range(HEADS):
        v = value[:, HEAD * h : HEAD * (h + 1)]
        doubled.append(cat(v, v, axis=0))
        l_send[h] = pack(dot(h_ref[h], doubled[h]))
    l_in = []
    for d in range(1, ROW):
        to = (place + d) % ROW
        l_in.append(copy_to(l_send.at[to], l_row.at[place], at_seq(y * ROW + to)))
    l_row[place] = l_send[place]
    column_chain()
    chain = z_chain[...][:, : ROW * HEAD]
    row_total = cat(*split(chain), axis=0)
    for entry in l_in:
        arrived(entry)
    lows = l_row[...].reshape(ROW * HEAD, 2 * HEAD)
    total = fold(dot(row_total, lows))
    t_send[...] = pack(total[:HEAD] + total[HEAD:])
    first = len(conditional)
    for d in range(1, NY):
        n = next(counter)
        conditional.append(
            (d, n, pltpu.make_async_remote_copy(
                src_ref=t_send, dst_ref=t_col.at[y], send_sem=send.at[n], recv_sem=recv.at[n],
                device_id=chip((y + d) % NY, x), device_id_type=MESH,
            ))
        )

        @pl.when(y + d < NY)
        def _(copy=conditional[-1][2]):
            copy.start()

    wide = ROW * HEAD
    span = z_all.shape[2] // 2
    from_row = []
    for j in range(ROW):
        both = cat(z_all[j, :, :wide], z_all[j, :, span : span + wide], axis=1)
        from_row.append(dot(both, cat(lows, lows, axis=0)))
    reads = [dot(y_ref[h], doubled[h]) for h in range(HEADS)]
    extra = coef_ref[...] * value.astype(F32)
    gate = gate_ref[...].astype(F32)

    for d, _, copy in conditional[first:]:

        @pl.when(y >= d)
        def _(copy=copy):
            copy.wait_recv()

    entering = fold(dot(z_row[...], t_col[...].reshape(NY * HEAD, 2 * HEAD)))
    entering = pack(entering[:HEAD] + entering[HEAD:])
    twice = cat(entering, entering, axis=0)
    for j in range(ROW):
        both = cat(
            z_all[j, :, wide : wide + HEAD], z_all[j, :, span + wide : span + wide + HEAD], axis=1
        )
        s_send[j] = pack(fold(from_row[j] + dot(both, twice)))
    s_wait = []
    for d in range(1, ROW):
        to = (place + d) % ROW
        s_wait.append(copy_to(s_send.at[to], s_in.at[place], at_seq(y * ROW + to)))
    s_in[place] = s_send[place]
    for entry in s_wait:
        arrived(entry)
    for h in range(HEADS):
        state = s_in[h]
        reads[h] = reads[h] + fold(dot(q_ref[h], cat(state, state, axis=0)))
    read = cat(*reads, axis=1)
    centre = read - head_sums(read) * (1.0 / HEAD)
    spread = head_sums(centre * centre) * (1.0 / HEAD)
    normed = centre * lax.rsqrt(spread + NORM_EPS) * scale_ref[...] + offset_ref[...]
    out_ref[...] = ((normed + extra) * gate).astype(BF16)

    finish()


COPIES = 128
SCRATCH = (
    pltpu.VMEM((TOKENS, WIDTH), BF16),
    pltpu.VMEM((TOKENS, WIDTH), BF16),
    pltpu.VMEM((TOKENS, WIDTH), BF16),
    pltpu.VMEM((TOKENS, WIDTH), BF16),
    pltpu.VMEM((TOKENS, WIDTH), F32),
    pltpu.VMEM((TOKENS, WIDTH), BF16),
    pltpu.VMEM((HEADS, TOKENS, 2 * TOKENS), BF16),
    pltpu.VMEM((HEADS, TOKENS, 2 * HEAD), BF16),
    pltpu.VMEM((HEADS, HEAD, 2 * TOKENS), BF16),
    pltpu.VMEM((HEADS, HEAD, 2 * HEAD), BF16),
    pltpu.VMEM((TOKENS, WIDTH), F32),
    pltpu.VMEM((16, WIDTH), BF16),
    pltpu.VMEM((TOKENS, 256), BF16),
    pltpu.VMEM((NZ, 2, TOKENS, 256), BF16),
    pltpu.VMEM((NY, NX, HEAD, 256), BF16),
    pltpu.VMEM((NY, NX, HEAD, 256), BF16),
    pltpu.VMEM((2, TOKENS, 256), F32),
    pltpu.VMEM((2, TOKENS, 256), F32),
    pltpu.VMEM((ROW, HEAD, 2 * HEAD), BF16),
    pltpu.VMEM((NY, HEAD, 2 * HEAD), BF16),
    pltpu.VMEM((HEAD, 640), F32),
    pltpu.VMEM((ROW, HEAD, 2 * 640), BF16),
    pltpu.VMEM((2 * HEAD, NY * HEAD), BF16),
    pltpu.VMEM((HEADS, HEAD, 2 * HEAD), BF16),
    pltpu.VMEM((ROW, HEAD, 2 * HEAD), BF16),
    pltpu.VMEM((HEAD, 2 * HEAD), BF16),
    pltpu.VMEM((NY, HEAD, 2 * HEAD), BF16),
    pltpu.VMEM((ROW, HEAD, 2 * HEAD), BF16),
    pltpu.VMEM((HEADS, HEAD, 2 * HEAD), BF16),
    pltpu.SemaphoreType.DMA((COPIES,)),
    pltpu.SemaphoreType.DMA((COPIES,)),
    pltpu.SemaphoreType.DMA((8,)),
)


def shards(
    activation_entries,
    content_mapping_matrix,
    content_lagged_blend,
    acceptance_vectors,
    address_vectors_given,
    inline_adaptation_speed,
    memory_fading_factors,
    result_filter_given,
    extra_coordinate_factors,
    group_layernorm_scaling,
    group_layernorm_offset,
):
    vmem = pl.BlockSpec(memory_space=pltpu.VMEM)

    def row(vector):
        return vector.reshape(1, WIDTH)

    hbm = pl.BlockSpec(memory_space=pl.ANY)
    return pl.pallas_call(
        time_mix,
        out_shape=jax.ShapeDtypeStruct((TOKENS, WIDTH), BF16),
        in_specs=[hbm] * 7 + [vmem] * 4,
        out_specs=vmem,
        scratch_shapes=SCRATCH,
        compiler_params=pltpu.CompilerParams(
            collective_id=0, has_side_effects=True, vmem_limit_bytes=56 << 20
        ),
        name="time_mix",
    )(
        activation_entries,
        content_mapping_matrix,
        acceptance_vectors,
        address_vectors_given,
        inline_adaptation_speed,
        memory_fading_factors,
        result_filter_given,
        row(content_lagged_blend),
        row(extra_coordinate_factors),
        row(group_layernorm_scaling),
        row(group_layernorm_offset),
    )


def solution(mesh):
    return jax.shard_map(
        shards,
        mesh=mesh,
        in_specs=(
            P("seq", "fsdp"),
            P("seq", "fsdp"),
            P("fsdp"),
            P("seq", "fsdp"),
            P("seq", "fsdp"),
            P("seq", "fsdp"),
            P("seq", "fsdp"),
            P("seq", "fsdp"),
            P("fsdp"),
            P("fsdp"),
            P("fsdp"),
        ),
        out_specs=P("seq", "fsdp"),
        check_vma=False,
    )
```

```python
import functools

import jax
import jax.numpy as jnp
from jax import lax
from jax.experimental import pallas as pl
from jax.experimental.pallas import tpu as pltpu
from jax.sharding import PartitionSpec as P

MESH = pl.DeviceIdType.MESH
F32 = jnp.float32
BF16 = jnp.bfloat16
HEAD = 64
HEADS = 8
TOKENS = 128
WIDTH = HEAD * HEADS
NX, NY, NZ = 4, 8, 8
ROW = 2 * NX
OFFSETS = (0, -1, 1, -2, 2, -3, 3, 4)
SLOT = {offset: n for n, offset in enumerate(OFFSETS)} | {-4: 7}
FAR_FIRST = (4, 3, 5, 2, 6, 1, 7)
NORM_EPS = 0.00064
UNIT_EPS = 1e-05


def split(x):
    high = x.astype(BF16)
    return high, (x - high.astype(F32)).astype(BF16)


def cat(*parts, axis):
    return jnp.concatenate(parts, axis=axis)


def dot(a, b):
    return jnp.dot(a, b, preferred_element_type=F32)


def dot_nt(a, b):
    return lax.dot_general(a, b, (((1,), (1,)), ((), ())), preferred_element_type=F32)


def wide_left(high, low):
    return cat(high, low, high, axis=1)


def wide_right(high, low):
    return cat(high, high, low, axis=0)


def iota(shape, dim):
    return lax.broadcasted_iota(jnp.int32, shape, dim)


def head_sums(x):
    ones = ((iota((256, 256), 0) // HEAD) == (iota((256, 256), 1) // HEAD)).astype(BF16)
    high, low = split(x)
    sums = dot(cat(high[:, :256], high[:, 256:], axis=0), ones) + dot(
        cat(low[:, :256], low[:, 256:], axis=0), ones
    )
    return cat(sums[:TOKENS], sums[TOKENS:], axis=1)


def shift_rows(x, steps, fill):
    rows = iota(x.shape, 0)
    return jnp.where(rows < steps, fill, pltpu.roll(x, steps, 0))


def prepare(r_ref, k_ref, a_ref, w_ref, bonus_ref, y_ref, q_ref, h_ref, g_ref, coef_ref):
    r = r_ref[...].astype(F32)
    k = k_ref[...].astype(F32)
    a = a_ref[...].astype(F32)
    unit = k * lax.rsqrt(head_sums(k * k) + UNIT_EPS)
    coef_ref[...] = head_sums(r * k * bonus_ref[...])
    cumul = w_ref[...]
    for level in range(7):
        cumul = cumul * shift_rows(cumul, 1 << level, 1.0)
    yield
    before = shift_rows(cumul, 1, 1.0)
    inverse = 1.0 / cumul
    end = cumul[TOKENS - 1 :, :]
    erase = -unit * before
    write = unit * a * inverse
    key = k * inverse
    rec = r * cumul
    erase_h, erase_l = split(erase)
    write_h, write_l = split(write)
    key_h, key_l = split(key)
    rec_h, rec_l = split(rec)
    write_end = write * end
    key_end = key * end
    rows, cols = iota((TOKENS, TOKENS), 0), iota((TOKENS, TOKENS), 1)
    strict, inclusive = rows > cols, rows >= cols
    differ = rows ^ cols
    eye = (rows == cols).astype(F32)
    small_eye = iota((HEAD, HEAD), 0) == iota((HEAD, HEAD), 1)

    grams, solves = [], []
    for h in range(HEADS):
        at = slice(HEAD * h, HEAD * (h + 1))
        left = wide_left(
            cat(erase_h[:, at], rec_h[:, at], axis=0), cat(erase_l[:, at], rec_l[:, at], axis=0)
        )
        high = cat(write_h[:, at], key_h[:, at], axis=0)
        low = cat(write_l[:, at], key_l[:, at], axis=0)
        grams.append(dot_nt(left, cat(high, high, low, axis=1)))
        if h == HEADS // 2 - 1:
            yield
    systems = [jnp.where(strict, gram[:TOKENS, :TOKENS], 0.0) for gram in grams]
    halves = [split(system) for system in systems]
    for h in range(HEADS):
        solves.append(eye + jnp.where(differ == 1, systems[h], 0.0))
    yield
    for level in range(1, 7):
        mask = (differ >> level) == 1
        for h in range(HEADS):
            rough = solves[h].astype(BF16)
            part = jnp.where(mask, halves[h][0], jnp.zeros_like(halves[h][0]))
            solves[h] = solves[h] + dot(rough, dot(part, rough).astype(BF16))
        yield
    for h in range(HEADS):
        high, low = split(solves[h])
        left_over = eye - solves[h] + dot(wide_left(*halves[h]), wide_right(high, low))
        solves[h] = solves[h] + dot(high, left_over.astype(BF16))
    yield
    inverses = [wide_left(*split(solve)) for solve in solves]
    mixes = []
    for pair in range(HEADS // 2):
        wide = slice(2 * HEAD * pair, 2 * HEAD * (pair + 1))
        write_t = write_end[:, wide].T
        for half in range(2):
            h = 2 * pair + half
            at = slice(HEAD * h, HEAD * (h + 1))
            keyed = dot(inverses[h], wide_right(erase_h[:, at], erase_l[:, at]))
            read_write = jnp.where(inclusive, grams[h][TOKENS:, :TOKENS], 0.0)
            mine = slice(HEAD * half, HEAD * (half + 1))
            mixes.append(wide_left(*split(cat(read_write, write_t[mine], axis=0))))
            out = dot(mixes[h], wide_right(*split(keyed)))
            q_ref[h] = cat(*split(rec[:, at] + out[:TOKENS]), axis=1)
            diagonal = jnp.where(small_eye, end[:, at], 0.0)
            g_ref[h] = cat(*split(diagonal + out[TOKENS:]), axis=1)
        if pair % 2:
            yield
    for pair in range(HEADS // 2):
        wide = slice(2 * HEAD * pair, 2 * HEAD * (pair + 1))
        key_t = key_end[:, wide].T
        for half in range(2):
            h = 2 * pair + half
            gram = grams[h]
            erase_key = jnp.where(strict, gram[:TOKENS, TOKENS:], 0.0)
            read_key = jnp.where(inclusive, gram[TOKENS:, TOKENS:], 0.0)
            valued = dot(inverses[h], wide_right(*split(erase_key)))
            out = dot(mixes[h], wide_right(*split(valued)))
            mine = slice(HEAD * half, HEAD * (half + 1))
            y_ref[h] = cat(*split(read_key + out[:TOKENS]), axis=1)
            h_ref[h] = cat(*split(key_t[mine] + out[TOKENS:]), axis=1)
        if pair % 2:
            yield


def chain_step(g, z):
    high, low = split(z)
    return dot(cat(g, g[:, :HEAD], axis=1), wide_right(high, low))


def fold(x):
    return x[:, :HEAD] + x[:, HEAD:]


def pack(x):
    return cat(*split(x), axis=1)


def time_mix(
    x_hbm, w_ref, r_hbm, k_hbm, a_hbm, decay_hbm, gate_hbm, blend_ref, bonus_ref, scale_ref, offset_ref,
    out_ref,
    x_ref, r_ref, k_ref, a_ref, decay_ref, gate_ref,
    y_ref, q_ref, h_ref, g_ref, coef_ref,
    prev_buf, x_send, xg, wa, wb, p_send, p_recv,
    g_row, g_col, z_chain, z_all, z_row,
    l_send, l_row, t_send, t_col, s_send, s_in,
    send, recv, local,
):
    s, z = lax.axis_index("seq"), lax.axis_index("fsdp")
    count = NX * NY * 2
    core, x, y, place = s % 2, (s // 2) % NX, s // ROW, s % ROW
    counter = iter(range(10**6))
    waiting, conditional = [], []

    def at_seq(index):
        return {"seq": index}

    def chip(yy, xx):
        return at_seq((yy * NX + xx) * 2 + core)

    def copy_to(source, target, device):
        n = next(counter)
        copy = pltpu.make_async_remote_copy(
            src_ref=source, dst_ref=target, send_sem=send.at[n], recv_sem=recv.at[n],
            device_id=device, device_id_type=MESH,
        )
        copy.start()
        entry = [copy, False]
        waiting.append(entry)
        return entry

    def arrived(entry):
        if not entry[1]:
            entry[1] = True
            entry[0].wait_recv()

    def arrived_from_below(number=None):
        for entry in conditional[:number]:
            if not entry[1]:
                entry[1] = True

                @pl.when(y >= entry[0])
                def _(copy=entry[2]):
                    copy.wait_recv()

    def finish():
        for entry in waiting:
            entry[0].wait_send()
        for d, _, copy in conditional:

            @pl.when(y + d < NY)
            def _(copy=copy):
                copy.wait_send()

    mate = at_seq(s + 1 - 2 * core)
    sides = (1, -1)
    barrier = pltpu.get_barrier_semaphore()
    partners = [chip(y, (x + d) % NX) for d in range(1, NX)]
    partners += [chip((y + NY + side) % NY, x) for side in sides]
    partners += [{"fsdp": (z + NZ + side) % NZ} for side in sides]
    partners += [mate, at_seq((s + count - 1 + 2 * core) % count)]
    for partner in partners:
        pl.semaphore_signal(barrier, inc=1, device_id=partner, device_id_type=MESH)
    own_a, own_b = w_ref.at[:, pl.ds(0, 256)], w_ref.at[:, pl.ds(256, 256)]
    loads = [
        pltpu.make_async_copy(source, target, local.at[n])
        for n, (source, target) in enumerate(
            (
                (x_hbm, x_ref),
                (own_a, wa.at[0, x]),
                (own_b, wb.at[0, x]),
                (r_hbm, r_ref),
                (k_hbm, k_ref),
                (a_hbm, a_ref),
                (decay_hbm, decay_ref),
                (gate_hbm, gate_ref),
            )
        )
    ]
    for load in loads:
        load.start()
    for d in range(NY):
        t_col[d] = jnp.zeros((HEAD, 2 * HEAD), BF16)
    pl.semaphore_wait(barrier, len(partners))

    yb, ya, zx = {}, {}, {}

    def row_at(offset):
        return (y + offset + NY) % NY

    def send_yb(step):
        if step > 1:
            for side in sides:
                arrived(yb[side, step - 1])
        for side in sides:
            source = own_b if step == 1 else wb.at[SLOT[-side * (step - 1)], x]
            yb[side, step] = copy_to(source, wb.at[SLOT[-side * step], x], chip(row_at(side), x))
            if step == 3 and side > 0:
                yb[side, 4] = copy_to(
                    wb.at[SLOT[-2 * side], x], wb.at[SLOT[4], x], chip(row_at(2 * side), x)
                )

    def send_xb(first, number):
        part = wb.at[pl.ds(first, number), x]
        for d in (2, 1, 3):
            copy_to(part, part, chip(y, (x + d) % NX))

    def send_zx(step, sub):
        part = core if sub == 0 else 1 - core
        if step > 1:
            for side in sides:
                arrived(zx[side, step - 1, sub])
        for side in sides:
            block = (z + NZ - side * (step - 1)) % NZ
            held = xg.at[block, part]
            if step == 3 and side == sides[sub]:
                zx[side, 4, sub] = copy_to(held, held, {"fsdp": (z + NZ + 2 * side) % NZ})
            zx[side, step, sub] = copy_to(held, held, {"fsdp": (z + NZ + side) % NZ})

    def send_ya(step, sub):
        if step > 1:
            for side in sides:
                arrived(ya[side, step - 1, sub])
        pair = pl.ds(2 * sub, 2)
        for side in sides:
            source = wa.at[SLOT[-side * (step - 1)], pair]
            if step == 3 and side == sides[sub]:
                ya[side, 4, sub] = copy_to(
                    source, wa.at[SLOT[4], pair], chip(row_at(2 * side), x)
                )
            ya[side, step, sub] = copy_to(
                source, wa.at[SLOT[-side * step], pair], chip(row_at(side), x)
            )

    def row_chain():
        for entry in g_in:
            arrived(entry)
        wide = z_chain.shape[1]
        lane, line = iota((HEAD, wide), 1), iota((HEAD, wide), 0)
        chain = (lane == line + ROW * HEAD).astype(F32)
        for j in range(ROW):
            z_all[j] = cat(*split(chain), axis=1)
            chain = chain_step(g_row[j], chain) + (lane == line + j * HEAD).astype(F32)
        z_chain[...] = chain

    def send_g_col():
        total = pack(z_chain[...][:, ROW * HEAD : (ROW + 1) * HEAD])
        g_col[y] = total
        for d in FAR_FIRST:
            n = next(counter)
            conditional.append(
                [d, False, pltpu.make_async_remote_copy(
                    src_ref=g_col.at[y], dst_ref=g_col.at[y], send_sem=send.at[n], recv_sem=recv.at[n],
                    device_id=chip((y + d) % NY, x), device_id_type=MESH,
                )]
            )

            @pl.when(y + d < NY)
            def _(copy=conditional[-1][2]):
                copy.start()

    def column_chain():
        arrived_from_below(NY - 1)
        lane, line = iota((HEAD, NY * HEAD), 1), iota((HEAD, NY * HEAD), 0)
        chain = jnp.zeros((HEAD, NY * HEAD), F32)
        for q in range(NY - 1):
            longer = chain_step(g_col[q], chain) + (lane == line + q * HEAD).astype(F32)
            chain = jnp.where(q < y, longer, chain)
        z_row[...] = cat(*split(chain), axis=0)

    stages = prepare(
        r_ref, k_ref, a_ref, decay_ref, bonus_ref, y_ref, q_ref, h_ref, g_ref, coef_ref
    )

    def compute(steps=1):
        for _ in range(steps):
            next(stages, None)

    a_in = [copy_to(own_a, wa.at[0, x], chip(y, (x + d) % NX)) for d in (2, 1, 3)]
    prev = copy_to(x_hbm.at[pl.ds(TOKENS - 16, 16)], prev_buf, at_seq((s + 1) % count))
    send_yb(1)
    for load in loads:
        load.wait()
    compute()

    arrived(prev)
    own = x_ref[...].astype(F32)
    before = jnp.where(s == 0, 0.0, prev_buf[...].astype(F32)[15:16, :])
    shifted = jnp.where(iota((TOKENS, WIDTH), 0) == 0, before, pltpu.roll(own, 1, 0))
    mixed = own + (shifted - own) * blend_ref[...]
    even = cat(*[mixed[:, 128 * q : 128 * q + 64] for q in range(4)], axis=1).astype(BF16)
    odd = cat(*[mixed[:, 128 * q + 64 : 128 * q + 128] for q in range(4)], axis=1).astype(BF16)
    is_even = core == 0
    xg[z, core] = jnp.where(is_even, even, odd)
    x_send[...] = jnp.where(is_even, odd, even)
    mate_x = copy_to(x_send, xg.at[z, core], mate)
    send_zx(1, 0)
    for entry in a_in:
        arrived(entry)
    send_ya(1, 0)
    send_ya(1, 1)
    arrived(mate_x)
    send_zx(1, 1)
    send_yb(2)
    send_xb(0, 3)
    compute(2)
    send_zx(2, 0)
    send_ya(2, 0)
    send_zx(2, 1)
    send_ya(2, 1)
    send_yb(3)
    send_xb(3, 2)
    compute(3)
    send_zx(3, 0)
    send_ya(3, 0)
    send_zx(3, 1)
    send_ya(3, 1)
    for side, step in ((1, 3), (-1, 3), (1, 4)):
        arrived(yb[side, step])
    send_xb(5, 3)
    compute(6)

    g_in = []
    for d in FAR_FIRST:
        to = (place + d) % ROW
        g_in.append(copy_to(g_ref.at[to], g_row.at[place], at_seq(y * ROW + to)))
    g_row[place] = g_ref[place]
    compute(100)
    for entry in waiting:
        if not any(entry is other for other in g_in):
            arrived(entry)
    parts = {}
    for mine in (False, True):
        block = core if mine else 1 - core
        for half, weights in enumerate((wa, wb)):
            total = jnp.zeros((TOKENS, 256), F32)
            for slot, offset in enumerate(OFFSETS):
                total = total + dot(xg[row_at(offset), block], weights[slot].reshape(256, 256))
            if mine:
                parts[half] = total
            else:
                p_send[half] = total
                parts[half, "copy"] = copy_to(p_send.at[half], p_recv.at[half], mate)
    values = []
    for half in range(2):
        arrived(parts[half, "copy"])
        values.append((parts[half] + p_recv[half]).astype(BF16))
    value = cat(*values, axis=1)

    doubled = []
    for h in range(HEADS):
        v = value[:, HEAD * h : HEAD * (h + 1)]
        doubled.append(cat(v, v, axis=0))
        l_send[h] = pack(dot(h_ref[h], doubled[h]))
    l_in = []
    for d in FAR_FIRST:
        to = (place + d) % ROW
        l_in.append(copy_to(l_send.at[to], l_row.at[place], at_seq(y * ROW + to)))
    l_row[place] = l_send[place]
    row_chain()
    send_g_col()
    chain = z_chain[...][:, : ROW * HEAD]
    row_total = cat(*split(chain), axis=0)
    for entry in l_in:
        arrived(entry)
    lows = l_row[...].reshape(ROW * HEAD, 2 * HEAD)
    total = fold(dot(row_total, lows))
    t_send[...] = pack(total[:HEAD] + total[HEAD:])
    for d in FAR_FIRST:
        n = next(counter)
        conditional.append(
            [d, False, pltpu.make_async_remote_copy(
                src_ref=t_send, dst_ref=t_col.at[y], send_sem=send.at[n], recv_sem=recv.at[n],
                device_id=chip((y + d) % NY, x), device_id_type=MESH,
            )]
        )

        @pl.when(y + d < NY)
        def _(copy=conditional[-1][2]):
            copy.start()

    wide = ROW * HEAD
    span = z_all.shape[2] // 2
    from_row = []
    for j in range(ROW):
        both = cat(z_all[j, :, :wide], z_all[j, :, span : span + wide], axis=1)
        from_row.append(dot(both, cat(lows, lows, axis=0)))
    reads = [dot(y_ref[h], doubled[h]) for h in range(HEADS)]
    extra = coef_ref[...] * value.astype(F32)
    gate = gate_ref[...].astype(F32)

    column_chain()
    arrived_from_below()
    entering = fold(dot(z_row[...], t_col[...].reshape(NY * HEAD, 2 * HEAD)))
    entering = pack(entering[:HEAD] + entering[HEAD:])
    twice = cat(entering, entering, axis=0)
    for j in range(ROW):
        both = cat(
            z_all[j, :, wide : wide + HEAD], z_all[j, :, span + wide : span + wide + HEAD], axis=1
        )
        s_send[j] = pack(fold(from_row[j] + dot(both, twice)))
    s_wait = []
    for d in FAR_FIRST:
        to = (place + d) % ROW
        s_wait.append(copy_to(s_send.at[to], s_in.at[place], at_seq(y * ROW + to)))
    s_in[place] = s_send[place]
    for entry in s_wait:
        arrived(entry)
    for h in range(HEADS):
        state = s_in[h]
        reads[h] = reads[h] + fold(dot(q_ref[h], cat(state, state, axis=0)))
    read = cat(*reads, axis=1)
    centre = read - head_sums(read) * (1.0 / HEAD)
    spread = head_sums(centre * centre) * (1.0 / HEAD)
    normed = centre * lax.rsqrt(spread + NORM_EPS) * scale_ref[...] + offset_ref[...]
    out_ref[...] = ((normed + extra) * gate).astype(BF16)

    finish()


COPIES = 128
SCRATCH = (
    pltpu.VMEM((TOKENS, WIDTH), BF16),
    pltpu.VMEM((TOKENS, WIDTH), BF16),
    pltpu.VMEM((TOKENS, WIDTH), BF16),
    pltpu.VMEM((TOKENS, WIDTH), BF16),
    pltpu.VMEM((TOKENS, WIDTH), F32),
    pltpu.VMEM((TOKENS, WIDTH), BF16),
    pltpu.VMEM((HEADS, TOKENS, 2 * TOKENS), BF16),
    pltpu.VMEM((HEADS, TOKENS, 2 * HEAD), BF16),
    pltpu.VMEM((HEADS, HEAD, 2 * TOKENS), BF16),
    pltpu.VMEM((HEADS, HEAD, 2 * HEAD), BF16),
    pltpu.VMEM((TOKENS, WIDTH), F32),
    pltpu.VMEM((16, WIDTH), BF16),
    pltpu.VMEM((TOKENS, 256), BF16),
    pltpu.VMEM((NZ, 2, TOKENS, 256), BF16),
    pltpu.VMEM((NY, NX, HEAD, 256), BF16),
    pltpu.VMEM((NY, NX, HEAD, 256), BF16),
    pltpu.VMEM((2, TOKENS, 256), F32),
    pltpu.VMEM((2, TOKENS, 256), F32),
    pltpu.VMEM((ROW, HEAD, 2 * HEAD), BF16),
    pltpu.VMEM((NY, HEAD, 2 * HEAD), BF16),
    pltpu.VMEM((HEAD, 640), F32),
    pltpu.VMEM((ROW, HEAD, 2 * 640), BF16),
    pltpu.VMEM((2 * HEAD, NY * HEAD), BF16),
    pltpu.VMEM((HEADS, HEAD, 2 * HEAD), BF16),
    pltpu.VMEM((ROW, HEAD, 2 * HEAD), BF16),
    pltpu.VMEM((HEAD, 2 * HEAD), BF16),
    pltpu.VMEM((NY, HEAD, 2 * HEAD), BF16),
    pltpu.VMEM((ROW, HEAD, 2 * HEAD), BF16),
    pltpu.VMEM((HEADS, HEAD, 2 * HEAD), BF16),
    pltpu.SemaphoreType.DMA((COPIES,)),
    pltpu.SemaphoreType.DMA((COPIES,)),
    pltpu.SemaphoreType.DMA((8,)),
)


def shards(
    activation_entries,
    content_mapping_matrix,
    content_lagged_blend,
    acceptance_vectors,
    address_vectors_given,
    inline_adaptation_speed,
    memory_fading_factors,
    result_filter_given,
    extra_coordinate_factors,
    group_layernorm_scaling,
    group_layernorm_offset,
):
    vmem = pl.BlockSpec(memory_space=pltpu.VMEM)

    def row(vector):
        return vector.reshape(1, WIDTH)

    hbm = pl.BlockSpec(memory_space=pl.ANY)
    return pl.pallas_call(
        time_mix,
        out_shape=jax.ShapeDtypeStruct((TOKENS, WIDTH), BF16),
        in_specs=[hbm] * 7 + [vmem] * 4,
        out_specs=vmem,
        scratch_shapes=SCRATCH,
        compiler_params=pltpu.CompilerParams(
            collective_id=0, has_side_effects=True, vmem_limit_bytes=56 << 20
        ),
        name="time_mix",
    )(
        activation_entries,
        content_mapping_matrix,
        acceptance_vectors,
        address_vectors_given,
        inline_adaptation_speed,
        memory_fading_factors,
        result_filter_given,
        row(content_lagged_blend),
        row(extra_coordinate_factors),
        row(group_layernorm_scaling),
        row(group_layernorm_offset),
    )


def solution(mesh):
    return jax.shard_map(
        shards,
        mesh=mesh,
        in_specs=(
            P("seq", "fsdp"),
            P("seq", "fsdp"),
            P("fsdp"),
            P("seq", "fsdp"),
            P("seq", "fsdp"),
            P("seq", "fsdp"),
            P("seq", "fsdp"),
            P("seq", "fsdp"),
            P("fsdp"),
            P("fsdp"),
            P("fsdp"),
        ),
        out_specs=P("seq", "fsdp"),
        check_vma=False,
    )
```

```python
import functools

import jax
import jax.numpy as jnp
from jax import lax
from jax.experimental import pallas as pl
from jax.experimental.pallas import tpu as pltpu
from jax.sharding import PartitionSpec as P

MESH = pl.DeviceIdType.MESH
F32 = jnp.float32
BF16 = jnp.bfloat16
HEAD = 64
HEADS = 8
TOKENS = 128
WIDTH = HEAD * HEADS
NX, NY, NZ = 4, 8, 8
ROW = 2 * NX
OFFSETS = (0, -1, 1, -2, 2, -3, 3, 4)
SLOT = {offset: n for n, offset in enumerate(OFFSETS)} | {-4: 7}
FAR_FIRST = (4, 3, 5, 2, 6, 1, 7)
NORM_EPS = 0.00064
UNIT_EPS = 1e-05


def split(x):
    high = x.astype(BF16)
    return high, (x - high.astype(F32)).astype(BF16)


def cat(*parts, axis):
    return jnp.concatenate(parts, axis=axis)


def dot(a, b):
    return jnp.dot(a, b, preferred_element_type=F32)


def dot_nt(a, b):
    return lax.dot_general(a, b, (((1,), (1,)), ((), ())), preferred_element_type=F32)


def wide_left(high, low):
    return cat(high, low, high, axis=1)


def wide_right(high, low):
    return cat(high, high, low, axis=0)


def iota(shape, dim):
    return lax.broadcasted_iota(jnp.int32, shape, dim)


def head_sums(x):
    ones = ((iota((256, 256), 0) // HEAD) == (iota((256, 256), 1) // HEAD)).astype(BF16)
    high, low = split(x)
    sums = dot(cat(high[:, :256], high[:, 256:], axis=0), ones) + dot(
        cat(low[:, :256], low[:, 256:], axis=0), ones
    )
    return cat(sums[:TOKENS], sums[TOKENS:], axis=1)


def shift_rows(x, steps, fill):
    rows = iota(x.shape, 0)
    return jnp.where(rows < steps, fill, pltpu.roll(x, steps, 0))


def prepare(r_ref, k_ref, a_ref, w_ref, bonus_ref, y_ref, q_ref, h_ref, g_ref, coef_ref):
    r = r_ref[...].astype(F32)
    k = k_ref[...].astype(F32)
    a = a_ref[...].astype(F32)
    unit = k * lax.rsqrt(head_sums(k * k) + UNIT_EPS)
    coef_ref[...] = head_sums(r * k * bonus_ref[...])
    cumul = w_ref[...]
    for level in range(7):
        cumul = cumul * shift_rows(cumul, 1 << level, 1.0)
    yield
    before = shift_rows(cumul, 1, 1.0)
    inverse = 1.0 / cumul
    end = cumul[TOKENS - 1 :, :]
    erase = -unit * before
    write = unit * a * inverse
    key = k * inverse
    rec = r * cumul
    erase_h, erase_l = split(erase)
    write_h, write_l = split(write)
    key_h, key_l = split(key)
    rec_h, rec_l = split(rec)
    write_end = write * end
    key_end = key * end
    rows, cols = iota((TOKENS, TOKENS), 0), iota((TOKENS, TOKENS), 1)
    strict, inclusive = rows > cols, rows >= cols
    differ = rows ^ cols
    eye = (rows == cols).astype(F32)
    small_eye = iota((HEAD, HEAD), 0) == iota((HEAD, HEAD), 1)

    grams, solves = [], []
    for h in range(HEADS):
        at = slice(HEAD * h, HEAD * (h + 1))
        left = wide_left(
            cat(erase_h[:, at], rec_h[:, at], axis=0), cat(erase_l[:, at], rec_l[:, at], axis=0)
        )
        high = cat(write_h[:, at], key_h[:, at], axis=0)
        low = cat(write_l[:, at], key_l[:, at], axis=0)
        grams.append(dot_nt(left, cat(high, high, low, axis=1)))
        if h == HEADS // 2 - 1:
            yield
    systems = [jnp.where(strict, gram[:TOKENS, :TOKENS], 0.0) for gram in grams]
    halves = [split(system) for system in systems]
    for h in range(HEADS):
        solves.append(eye + jnp.where(differ == 1, systems[h], 0.0))
    yield
    for level in range(1, 7):
        mask = (differ >> level) == 1
        for h in range(HEADS):
            rough = solves[h].astype(BF16)
            part = jnp.where(mask, halves[h][0], jnp.zeros_like(halves[h][0]))
            solves[h] = solves[h] + dot(rough, dot(part, rough).astype(BF16))
        yield
    for h in range(HEADS):
        high, low = split(solves[h])
        left_over = eye - solves[h] + dot(wide_left(*halves[h]), wide_right(high, low))
        solves[h] = solves[h] + dot(high, left_over.astype(BF16))
    yield
    inverses = [wide_left(*split(solve)) for solve in solves]
    mixes = []
    for pair in range(HEADS // 2):
        wide = slice(2 * HEAD * pair, 2 * HEAD * (pair + 1))
        write_t = write_end[:, wide].T
        for half in range(2):
            h = 2 * pair + half
            at = slice(HEAD * h, HEAD * (h + 1))
            keyed = dot(inverses[h], wide_right(erase_h[:, at], erase_l[:, at]))
            read_write = jnp.where(inclusive, grams[h][TOKENS:, :TOKENS], 0.0)
            mine = slice(HEAD * half, HEAD * (half + 1))
            mixes.append(wide_left(*split(cat(read_write, write_t[mine], axis=0))))
            out = dot(mixes[h], wide_right(*split(keyed)))
            q_ref[h] = cat(*split(rec[:, at] + out[:TOKENS]), axis=1)
            diagonal = jnp.where(small_eye, end[:, at], 0.0)
            g_ref[h] = cat(*split(diagonal + out[TOKENS:]), axis=1)
        if pair % 2:
            yield
    for pair in range(HEADS // 2):
        wide = slice(2 * HEAD * pair, 2 * HEAD * (pair + 1))
        key_t = key_end[:, wide].T
        for half in range(2):
            h = 2 * pair + half
            gram = grams[h]
            erase_key = jnp.where(strict, gram[:TOKENS, TOKENS:], 0.0)
            read_key = jnp.where(inclusive, gram[TOKENS:, TOKENS:], 0.0)
            valued = dot(inverses[h], wide_right(*split(erase_key)))
            out = dot(mixes[h], wide_right(*split(valued)))
            mine = slice(HEAD * half, HEAD * (half + 1))
            y_ref[h] = cat(*split(read_key + out[:TOKENS]), axis=1)
            h_ref[h] = cat(*split(key_t[mine] + out[TOKENS:]), axis=1)
        if pair % 2:
            yield


def chain_step(g, z):
    high, low = split(z)
    return dot(cat(g, g[:, :HEAD], axis=1), wide_right(high, low))


def fold(x):
    return x[:, :HEAD] + x[:, HEAD:]


def pack(x):
    return cat(*split(x), axis=1)


def time_mix(
    x_hbm, w_ref, r_hbm, k_hbm, a_hbm, decay_hbm, gate_hbm, blend_ref, bonus_ref, scale_ref, offset_ref,
    out_ref,
    x_ref, r_ref, k_ref, a_ref, decay_ref, gate_ref,
    y_ref, q_ref, h_ref, g_ref, coef_ref,
    prev_buf, x_send, xg, wa, wb, p_send, p_recv,
    g_row, g_col, z_chain, z_all, z_row,
    l_send, l_row, t_send, t_col, s_send, s_in,
    send, recv, local,
):
    s, z = lax.axis_index("seq"), lax.axis_index("fsdp")
    count = NX * NY * 2
    core, x, y, place = s % 2, (s // 2) % NX, s // ROW, s % ROW
    counter = iter(range(10**6))
    waiting, conditional = [], []

    def at_seq(index):
        return {"seq": index}

    def chip(yy, xx):
        return at_seq((yy * NX + xx) * 2 + core)

    def copy_to(source, target, device):
        n = next(counter)
        copy = pltpu.make_async_remote_copy(
            src_ref=source, dst_ref=target, send_sem=send.at[n], recv_sem=recv.at[n],
            device_id=device, device_id_type=MESH,
        )
        copy.start()
        entry = [copy, False]
        waiting.append(entry)
        return entry

    def arrived(entry):
        if not entry[1]:
            entry[1] = True
            entry[0].wait_recv()

    def arrived_from_below(number=None):
        for entry in conditional[:number]:
            if not entry[1]:
                entry[1] = True

                @pl.when(y >= entry[0])
                def _(copy=entry[2]):
                    copy.wait_recv()

    def finish():
        for entry in waiting:
            entry[0].wait_send()
        for d, _, copy in conditional:

            @pl.when(y + d < NY)
            def _(copy=copy):
                copy.wait_send()

    mate = at_seq(s + 1 - 2 * core)
    sides = (1, -1)
    barrier = pltpu.get_barrier_semaphore()
    partners = [chip(y, (x + d) % NX) for d in range(1, NX)]
    partners += [chip((y + NY + side) % NY, x) for side in sides]
    partners += [{"fsdp": (z + NZ + side) % NZ} for side in sides]
    partners += [mate, at_seq((s + count - 1 + 2 * core) % count)]
    for partner in partners:
        pl.semaphore_signal(barrier, inc=1, device_id=partner, device_id_type=MESH)
    own_a, own_b = w_ref.at[:, pl.ds(0, 256)], w_ref.at[:, pl.ds(256, 256)]
    loads = [
        pltpu.make_async_copy(source, target, local.at[n])
        for n, (source, target) in enumerate(
            (
                (x_hbm, x_ref),
                (own_a, wa.at[0, x]),
                (own_b, wb.at[0, x]),
                (r_hbm, r_ref),
                (k_hbm, k_ref),
                (a_hbm, a_ref),
                (decay_hbm, decay_ref),
                (gate_hbm, gate_ref),
            )
        )
    ]
    for load in loads:
        load.start()
    for d in range(NY):
        t_col[d] = jnp.zeros((HEAD, 2 * HEAD), BF16)
    pl.semaphore_wait(barrier, len(partners))

    yb, ya, zx = {}, {}, {}

    def row_at(offset):
        return (y + offset + NY) % NY

    def send_yb(step):
        if step > 1:
            for side in sides:
                arrived(yb[side, step - 1])
        for side in sides:
            source = own_b if step == 1 else wb.at[SLOT[-side * (step - 1)], x]
            yb[side, step] = copy_to(source, wb.at[SLOT[-side * step], x], chip(row_at(side), x))
            if step == 3 and side > 0:
                yb[side, 4] = copy_to(
                    wb.at[SLOT[-2 * side], x], wb.at[SLOT[4], x], chip(row_at(2 * side), x)
                )

    def send_xb(first, number):
        part = wb.at[pl.ds(first, number), x]
        for d in (2, 1, 3):
            if first == 0:
                copy_to(own_b, wb.at[0, x], chip(y, (x + d) % NX))
            else:
                copy_to(part, part, chip(y, (x + d) % NX))

    def send_zx(step, sub):
        part = core if sub == 0 else 1 - core
        if step > 1:
            for side in sides:
                arrived(zx[side, step - 1, sub])
        for side in sides:
            block = (z + NZ - side * (step - 1)) % NZ
            held = xg.at[block, part]
            if step == 3 and side == sides[sub]:
                zx[side, 4, sub] = copy_to(held, held, {"fsdp": (z + NZ + 2 * side) % NZ})
            zx[side, step, sub] = copy_to(held, held, {"fsdp": (z + NZ + side) % NZ})

    def send_ya(step, sub):
        if step > 1:
            for side in sides:
                arrived(ya[side, step - 1, sub])
        pair = pl.ds(2 * sub, 2)
        for side in sides:
            source = wa.at[SLOT[-side * (step - 1)], pair]
            if step == 3 and side == sides[sub]:
                ya[side, 4, sub] = copy_to(
                    source, wa.at[SLOT[4], pair], chip(row_at(2 * side), x)
                )
            ya[side, step, sub] = copy_to(
                source, wa.at[SLOT[-side * step], pair], chip(row_at(side), x)
            )

    def row_chain():
        for entry in g_in:
            arrived(entry)
        wide = z_chain.shape[1]
        lane, line = iota((HEAD, wide), 1), iota((HEAD, wide), 0)
        chain = (lane == line + ROW * HEAD).astype(F32)
        for j in range(ROW):
            z_all[j] = cat(*split(chain), axis=1)
            chain = chain_step(g_row[j], chain) + (lane == line + j * HEAD).astype(F32)
        z_chain[...] = chain

    def send_g_col():
        total = pack(z_chain[...][:, ROW * HEAD : (ROW + 1) * HEAD])
        g_col[y] = total
        for d in FAR_FIRST:
            n = next(counter)
            conditional.append(
                [d, False, pltpu.make_async_remote_copy(
                    src_ref=g_col.at[y], dst_ref=g_col.at[y], send_sem=send.at[n], recv_sem=recv.at[n],
                    device_id=chip((y + d) % NY, x), device_id_type=MESH,
                )]
            )

            @pl.when(y + d < NY)
            def _(copy=conditional[-1][2]):
                copy.start()

    def column_chain():
        arrived_from_below(NY - 1)
        lane, line = iota((HEAD, NY * HEAD), 1), iota((HEAD, NY * HEAD), 0)
        chain = jnp.zeros((HEAD, NY * HEAD), F32)
        for q in range(NY - 1):
            longer = chain_step(g_col[q], chain) + (lane == line + q * HEAD).astype(F32)
            chain = jnp.where(q < y, longer, chain)
        z_row[...] = cat(*split(chain), axis=0)

    stages = prepare(
        r_ref, k_ref, a_ref, decay_ref, bonus_ref, y_ref, q_ref, h_ref, g_ref, coef_ref
    )

    def compute(steps=1):
        for _ in range(steps):
            next(stages, None)

    a_in = [copy_to(own_a, wa.at[0, x], chip(y, (x + d) % NX)) for d in (2, 1, 3)]
    prev = copy_to(x_hbm.at[pl.ds(TOKENS - 16, 16)], prev_buf, at_seq((s + 1) % count))
    send_yb(1)
    send_xb(0, 1)
    for load in loads:
        load.wait()
    compute()

    arrived(prev)
    own = x_ref[...].astype(F32)
    before = jnp.where(s == 0, 0.0, prev_buf[...].astype(F32)[15:16, :])
    shifted = jnp.where(iota((TOKENS, WIDTH), 0) == 0, before, pltpu.roll(own, 1, 0))
    mixed = own + (shifted - own) * blend_ref[...]
    even = cat(*[mixed[:, 128 * q : 128 * q + 64] for q in range(4)], axis=1).astype(BF16)
    odd = cat(*[mixed[:, 128 * q + 64 : 128 * q + 128] for q in range(4)], axis=1).astype(BF16)
    is_even = core == 0
    xg[z, core] = jnp.where(is_even, even, odd)
    x_send[...] = jnp.where(is_even, odd, even)
    mate_x = copy_to(x_send, xg.at[z, core], mate)
    send_zx(1, 0)
    for entry in a_in:
        arrived(entry)
    send_ya(1, 0)
    send_ya(1, 1)
    arrived(mate_x)
    send_zx(1, 1)
    send_yb(2)
    send_xb(1, 2)
    compute(7)
    send_zx(2, 0)
    send_ya(2, 0)
    send_zx(2, 1)
    send_ya(2, 1)
    send_yb(3)
    send_xb(3, 2)
    compute(4)
    g_in = []
    for d in FAR_FIRST:
        to = (place + d) % ROW
        g_in.append(copy_to(g_ref.at[to], g_row.at[place], at_seq(y * ROW + to)))
    g_row[place] = g_ref[place]
    send_zx(3, 0)
    send_ya(3, 0)
    send_zx(3, 1)
    send_ya(3, 1)
    for side, step in ((1, 3), (-1, 3), (1, 4)):
        arrived(yb[side, step])
    send_xb(5, 3)
    compute(100)
    row_chain()
    send_g_col()
    for entry in list(zx.values()) + list(ya.values()):
        arrived(entry)

    partial = []
    for half, weights in enumerate((wa, wb)):
        if half:
            for entry in waiting[:-1]:
                arrived(entry)
        total = jnp.zeros((2 * TOKENS, 256), F32)
        for slot, offset in enumerate(OFFSETS):
            total = total + dot(
                xg[row_at(offset)].reshape(2 * TOKENS, 256), weights[slot].reshape(256, 256)
            )
        p_send[half] = total.reshape(2, TOKENS, 256)
        partial.append(copy_to(p_send.at[half, 1 - core], p_recv.at[half], mate))
    values = []
    for half in range(2):
        arrived(partial[half])
        values.append((p_send[half, core] + p_recv[half]).astype(BF16))
    value = cat(*values, axis=1)

    doubled = []
    for h in range(HEADS):
        v = value[:, HEAD * h : HEAD * (h + 1)]
        doubled.append(cat(v, v, axis=0))
        l_send[h] = pack(dot(h_ref[h], doubled[h]))
    l_in = []
    for d in FAR_FIRST:
        to = (place + d) % ROW
        l_in.append(copy_to(l_send.at[to], l_row.at[place], at_seq(y * ROW + to)))
    l_row[place] = l_send[place]
    chain = z_chain[...][:, : ROW * HEAD]
    row_total = cat(*split(chain), axis=0)
    for entry in l_in:
        arrived(entry)
    lows = l_row[...].reshape(ROW * HEAD, 2 * HEAD)
    total = fold(dot(row_total, lows))
    t_send[...] = pack(total[:HEAD] + total[HEAD:])
    for d in FAR_FIRST:
        n = next(counter)
        conditional.append(
            [d, False, pltpu.make_async_remote_copy(
                src_ref=t_send, dst_ref=t_col.at[y], send_sem=send.at[n], recv_sem=recv.at[n],
                device_id=chip((y + d) % NY, x), device_id_type=MESH,
            )]
        )

        @pl.when(y + d < NY)
        def _(copy=conditional[-1][2]):
            copy.start()

    wide = ROW * HEAD
    span = z_all.shape[2] // 2
    from_row = []
    for j in range(ROW):
        both = cat(z_all[j, :, :wide], z_all[j, :, span : span + wide], axis=1)
        from_row.append(dot(both, cat(lows, lows, axis=0)))
    reads = [dot(y_ref[h], doubled[h]) for h in range(HEADS)]
    extra = coef_ref[...] * value.astype(F32)
    gate = gate_ref[...].astype(F32)

    column_chain()
    arrived_from_below()
    entering = fold(dot(z_row[...], t_col[...].reshape(NY * HEAD, 2 * HEAD)))
    entering = pack(entering[:HEAD] + entering[HEAD:])
    twice = cat(entering, entering, axis=0)
    for j in range(ROW):
        both = cat(
            z_all[j, :, wide : wide + HEAD], z_all[j, :, span + wide : span + wide + HEAD], axis=1
        )
        s_send[j] = pack(fold(from_row[j] + dot(both, twice)))
    s_wait = []
    for d in FAR_FIRST:
        to = (place + d) % ROW
        s_wait.append(copy_to(s_send.at[to], s_in.at[place], at_seq(y * ROW + to)))
    s_in[place] = s_send[place]
    for entry in s_wait:
        arrived(entry)
    for h in range(HEADS):
        state = s_in[h]
        reads[h] = reads[h] + fold(dot(q_ref[h], cat(state, state, axis=0)))
    read = cat(*reads, axis=1)
    centre = read - head_sums(read) * (1.0 / HEAD)
    spread = head_sums(centre * centre) * (1.0 / HEAD)
    normed = centre * lax.rsqrt(spread + NORM_EPS) * scale_ref[...] + offset_ref[...]
    out_ref[...] = ((normed + extra) * gate).astype(BF16)

    finish()


COPIES = 128
SCRATCH = (
    pltpu.VMEM((TOKENS, WIDTH), BF16),
    pltpu.VMEM((TOKENS, WIDTH), BF16),
    pltpu.VMEM((TOKENS, WIDTH), BF16),
    pltpu.VMEM((TOKENS, WIDTH), BF16),
    pltpu.VMEM((TOKENS, WIDTH), F32),
    pltpu.VMEM((TOKENS, WIDTH), BF16),
    pltpu.VMEM((HEADS, TOKENS, 2 * TOKENS), BF16),
    pltpu.VMEM((HEADS, TOKENS, 2 * HEAD), BF16),
    pltpu.VMEM((HEADS, HEAD, 2 * TOKENS), BF16),
    pltpu.VMEM((HEADS, HEAD, 2 * HEAD), BF16),
    pltpu.VMEM((TOKENS, WIDTH), F32),
    pltpu.VMEM((16, WIDTH), BF16),
    pltpu.VMEM((TOKENS, 256), BF16),
    pltpu.VMEM((NZ, 2, TOKENS, 256), BF16),
    pltpu.VMEM((NY, NX, HEAD, 256), BF16),
    pltpu.VMEM((NY, NX, HEAD, 256), BF16),
    pltpu.VMEM((2, 2, TOKENS, 256), F32),
    pltpu.VMEM((2, TOKENS, 256), F32),
    pltpu.VMEM((ROW, HEAD, 2 * HEAD), BF16),
    pltpu.VMEM((NY, HEAD, 2 * HEAD), BF16),
    pltpu.VMEM((HEAD, 640), F32),
    pltpu.VMEM((ROW, HEAD, 2 * 640), BF16),
    pltpu.VMEM((2 * HEAD, NY * HEAD), BF16),
    pltpu.VMEM((HEADS, HEAD, 2 * HEAD), BF16),
    pltpu.VMEM((ROW, HEAD, 2 * HEAD), BF16),
    pltpu.VMEM((HEAD, 2 * HEAD), BF16),
    pltpu.VMEM((NY, HEAD, 2 * HEAD), BF16),
    pltpu.VMEM((ROW, HEAD, 2 * HEAD), BF16),
    pltpu.VMEM((HEADS, HEAD, 2 * HEAD), BF16),
    pltpu.SemaphoreType.DMA((COPIES,)),
    pltpu.SemaphoreType.DMA((COPIES,)),
    pltpu.SemaphoreType.DMA((8,)),
)


def shards(
    activation_entries,
    content_mapping_matrix,
    content_lagged_blend,
    acceptance_vectors,
    address_vectors_given,
    inline_adaptation_speed,
    memory_fading_factors,
    result_filter_given,
    extra_coordinate_factors,
    group_layernorm_scaling,
    group_layernorm_offset,
):
    vmem = pl.BlockSpec(memory_space=pltpu.VMEM)

    def row(vector):
        return vector.reshape(1, WIDTH)

    hbm = pl.BlockSpec(memory_space=pl.ANY)
    return pl.pallas_call(
        time_mix,
        out_shape=jax.ShapeDtypeStruct((TOKENS, WIDTH), BF16),
        in_specs=[hbm] * 7 + [vmem] * 4,
        out_specs=vmem,
        scratch_shapes=SCRATCH,
        compiler_params=pltpu.CompilerParams(
            collective_id=0, has_side_effects=True, vmem_limit_bytes=56 << 20
        ),
        name="time_mix",
    )(
        activation_entries,
        content_mapping_matrix,
        acceptance_vectors,
        address_vectors_given,
        inline_adaptation_speed,
        memory_fading_factors,
        result_filter_given,
        row(content_lagged_blend),
        row(extra_coordinate_factors),
        row(group_layernorm_scaling),
        row(group_layernorm_offset),
    )


def solution(mesh):
    return jax.shard_map(
        shards,
        mesh=mesh,
        in_specs=(
            P("seq", "fsdp"),
            P("seq", "fsdp"),
            P("fsdp"),
            P("seq", "fsdp"),
            P("seq", "fsdp"),
            P("seq", "fsdp"),
            P("seq", "fsdp"),
            P("seq", "fsdp"),
            P("fsdp"),
            P("fsdp"),
            P("fsdp"),
        ),
        out_specs=P("seq", "fsdp"),
        check_vma=False,
    )
```

```python
import functools

import jax
import jax.numpy as jnp
from jax import lax
from jax.experimental import pallas as pl
from jax.experimental.pallas import tpu as pltpu
from jax.sharding import PartitionSpec as P

MESH = pl.DeviceIdType.MESH
F32 = jnp.float32
BF16 = jnp.bfloat16
HEAD = 64
HEADS = 8
TOKENS = 128
WIDTH = HEAD * HEADS
NX, NY, NZ = 4, 8, 8
ROW = 2 * NX
OFFSETS = (0, -1, 1, -2, 2, -3, 3, 4)
SLOT = {offset: n for n, offset in enumerate(OFFSETS)} | {-4: 7}
FAR_FIRST = (4, 3, 5, 2, 6, 1, 7)
NORM_EPS = 0.00064
UNIT_EPS = 1e-05


def split(x):
    high = x.astype(BF16)
    return high, (x - high.astype(F32)).astype(BF16)


def cat(*parts, axis):
    return jnp.concatenate(parts, axis=axis)


def dot(a, b):
    return jnp.dot(a, b, preferred_element_type=F32)


def dot_nt(a, b):
    return lax.dot_general(a, b, (((1,), (1,)), ((), ())), preferred_element_type=F32)


def wide_left(high, low):
    return cat(high, low, high, axis=1)


def wide_right(high, low):
    return cat(high, high, low, axis=0)


def iota(shape, dim):
    return lax.broadcasted_iota(jnp.int32, shape, dim)


def head_sums(x):
    ones = ((iota((256, 256), 0) // HEAD) == (iota((256, 256), 1) // HEAD)).astype(BF16)
    high, low = split(x)
    sums = dot(cat(high[:, :256], high[:, 256:], axis=0), ones) + dot(
        cat(low[:, :256], low[:, 256:], axis=0), ones
    )
    return cat(sums[:TOKENS], sums[TOKENS:], axis=1)


def shift_rows(x, steps, fill):
    rows = iota(x.shape, 0)
    return jnp.where(rows < steps, fill, pltpu.roll(x, steps, 0))


def prepare(r_ref, k_ref, a_ref, w_ref, bonus_ref, y_ref, q_ref, h_ref, g_ref, coef_ref):
    r = r_ref[...].astype(F32)
    k = k_ref[...].astype(F32)
    a = a_ref[...].astype(F32)
    unit = k * lax.rsqrt(head_sums(k * k) + UNIT_EPS)
    coef_ref[...] = head_sums(r * k * bonus_ref[...])
    cumul = w_ref[...]
    for level in range(7):
        cumul = cumul * shift_rows(cumul, 1 << level, 1.0)
    yield
    before = shift_rows(cumul, 1, 1.0)
    inverse = 1.0 / cumul
    end = cumul[TOKENS - 1 :, :]
    erase = -unit * before
    write = unit * a * inverse
    key = k * inverse
    rec = r * cumul
    erase_h, erase_l = split(erase)
    write_h, write_l = split(write)
    key_h, key_l = split(key)
    rec_h, rec_l = split(rec)
    write_end = write * end
    key_end = key * end
    rows, cols = iota((TOKENS, TOKENS), 0), iota((TOKENS, TOKENS), 1)
    strict, inclusive = rows > cols, rows >= cols
    differ = rows ^ cols
    eye = (rows == cols).astype(F32)
    small_eye = iota((HEAD, HEAD), 0) == iota((HEAD, HEAD), 1)

    grams, solves = [], []
    for h in range(HEADS):
        at = slice(HEAD * h, HEAD * (h + 1))
        left = wide_left(
            cat(erase_h[:, at], rec_h[:, at], axis=0), cat(erase_l[:, at], rec_l[:, at], axis=0)
        )
        high = cat(write_h[:, at], key_h[:, at], axis=0)
        low = cat(write_l[:, at], key_l[:, at], axis=0)
        grams.append(dot_nt(left, cat(high, high, low, axis=1)))
        if h == HEADS // 2 - 1:
            yield
    systems = [jnp.where(strict, gram[:TOKENS, :TOKENS], 0.0) for gram in grams]
    halves = [split(system) for system in systems]
    for h in range(HEADS):
        solves.append(eye + jnp.where(differ == 1, systems[h], 0.0))
    yield
    for level in range(1, 7):
        mask = (differ >> level) == 1
        for h in range(HEADS):
            rough = solves[h].astype(BF16)
            part = jnp.where(mask, halves[h][0], jnp.zeros_like(halves[h][0]))
            solves[h] = solves[h] + dot(rough, dot(part, rough).astype(BF16))
        yield
    for h in range(HEADS):
        high, low = split(solves[h])
        left_over = eye - solves[h] + dot(wide_left(*halves[h]), wide_right(high, low))
        solves[h] = solves[h] + dot(high, left_over.astype(BF16))
    yield
    inverses = [wide_left(*split(solve)) for solve in solves]
    mixes = []
    for pair in range(HEADS // 2):
        wide = slice(2 * HEAD * pair, 2 * HEAD * (pair + 1))
        write_t = write_end[:, wide].T
        for half in range(2):
            h = 2 * pair + half
            at = slice(HEAD * h, HEAD * (h + 1))
            keyed = dot(inverses[h], wide_right(erase_h[:, at], erase_l[:, at]))
            read_write = jnp.where(inclusive, grams[h][TOKENS:, :TOKENS], 0.0)
            mine = slice(HEAD * half, HEAD * (half + 1))
            mixes.append(wide_left(*split(cat(read_write, write_t[mine], axis=0))))
            out = dot(mixes[h], wide_right(*split(keyed)))
            q_ref[h] = cat(*split(rec[:, at] + out[:TOKENS]), axis=1)
            diagonal = jnp.where(small_eye, end[:, at], 0.0)
            g_ref[h] = cat(*split(diagonal + out[TOKENS:]), axis=1)
        if pair % 2:
            yield
    for pair in range(HEADS // 2):
        wide = slice(2 * HEAD * pair, 2 * HEAD * (pair + 1))
        key_t = key_end[:, wide].T
        for half in range(2):
            h = 2 * pair + half
            gram = grams[h]
            erase_key = jnp.where(strict, gram[:TOKENS, TOKENS:], 0.0)
            read_key = jnp.where(inclusive, gram[TOKENS:, TOKENS:], 0.0)
            valued = dot(inverses[h], wide_right(*split(erase_key)))
            out = dot(mixes[h], wide_right(*split(valued)))
            mine = slice(HEAD * half, HEAD * (half + 1))
            y_ref[h] = cat(*split(read_key + out[:TOKENS]), axis=1)
            h_ref[h] = cat(*split(key_t[mine] + out[TOKENS:]), axis=1)
        if pair % 2:
            yield


def chain_step(g, z):
    high, low = split(z)
    return dot(cat(g, g[:, :HEAD], axis=1), wide_right(high, low))


def fold(x):
    return x[:, :HEAD] + x[:, HEAD:]


def pack(x):
    return cat(*split(x), axis=1)


def time_mix(
    x_hbm, w_ref, r_hbm, k_hbm, a_hbm, decay_hbm, gate_hbm, blend_ref, bonus_ref, scale_ref, offset_ref,
    out_ref,
    x_ref, r_ref, k_ref, a_ref, decay_ref, gate_ref,
    y_ref, q_ref, h_ref, g_ref, coef_ref,
    prev_buf, x_send, xg, wa, wb, p_send, p_recv,
    g_row, g_col, z_chain, z_all, p_all, z_row,
    l_send, l_row, t_send, t_col, s_send, s_in,
    send, recv, local,
):
    s, z = lax.axis_index("seq"), lax.axis_index("fsdp")
    count = NX * NY * 2
    core, x, y, place = s % 2, (s // 2) % NX, s // ROW, s % ROW
    counter = iter(range(10**6))
    waiting, conditional = [], []

    def at_seq(index):
        return {"seq": index}

    def chip(yy, xx):
        return at_seq((yy * NX + xx) * 2 + core)

    def copy_to(source, target, device):
        n = next(counter)
        copy = pltpu.make_async_remote_copy(
            src_ref=source, dst_ref=target, send_sem=send.at[n], recv_sem=recv.at[n],
            device_id=device, device_id_type=MESH,
        )
        copy.start()
        entry = [copy, False]
        waiting.append(entry)
        return entry

    def arrived(entry):
        if not entry[1]:
            entry[1] = True
            entry[0].wait_recv()

    def arrived_from_below(number=None):
        for entry in conditional[:number]:
            if not entry[1]:
                entry[1] = True

                @pl.when(y >= entry[0])
                def _(copy=entry[2]):
                    copy.wait_recv()

    def finish():
        for entry in waiting:
            entry[0].wait_send()
        for d, _, copy in conditional:

            @pl.when(y + d < NY)
            def _(copy=copy):
                copy.wait_send()

    mate = at_seq(s + 1 - 2 * core)
    sides = (1, -1)
    barrier = pltpu.get_barrier_semaphore()
    partners = [chip(y, (x + d) % NX) for d in range(1, NX)]
    partners += [chip((y + NY + side) % NY, x) for side in sides]
    partners += [{"fsdp": (z + NZ + side) % NZ} for side in sides]
    partners += [mate, at_seq((s + count - 1 + 2 * core) % count)]
    for partner in partners:
        pl.semaphore_signal(barrier, inc=1, device_id=partner, device_id_type=MESH)
    own_a, own_b = w_ref.at[:, pl.ds(0, 256)], w_ref.at[:, pl.ds(256, 256)]
    loads = [
        pltpu.make_async_copy(source, target, local.at[n])
        for n, (source, target) in enumerate(
            (
                (x_hbm, x_ref),
                (own_a, wa.at[0, x]),
                (own_b, wb.at[0, x]),
                (r_hbm, r_ref),
                (k_hbm, k_ref),
                (a_hbm, a_ref),
                (decay_hbm, decay_ref),
                (gate_hbm, gate_ref),
            )
        )
    ]
    for load in loads:
        load.start()
    for d in range(NY):
        t_col[d] = jnp.zeros((HEAD, 2 * HEAD), BF16)
    pl.semaphore_wait(barrier, len(partners))

    yb, ya, zx = {}, {}, {}

    def row_at(offset):
        return (y + offset + NY) % NY

    def send_yb(step):
        if step > 1:
            for side in sides:
                arrived(yb[side, step - 1])
        for side in sides:
            source = own_b if step == 1 else wb.at[SLOT[-side * (step - 1)], x]
            yb[side, step] = copy_to(source, wb.at[SLOT[-side * step], x], chip(row_at(side), x))
            if step == 3 and side > 0:
                yb[side, 4] = copy_to(
                    wb.at[SLOT[-2 * side], x], wb.at[SLOT[4], x], chip(row_at(2 * side), x)
                )

    def send_xb(first, number):
        part = wb.at[pl.ds(first, number), x]
        for d in (2, 1, 3):
            if first == 0:
                copy_to(own_b, wb.at[0, x], chip(y, (x + d) % NX))
            else:
                copy_to(part, part, chip(y, (x + d) % NX))

    def send_zx(step, sub):
        part = core if sub == 0 else 1 - core
        if step > 1:
            for side in sides:
                arrived(zx[side, step - 1, sub])
        for side in sides:
            block = (z + NZ - side * (step - 1)) % NZ
            held = xg.at[block, part]
            if step == 3 and side == sides[sub]:
                zx[side, 4, sub] = copy_to(held, held, {"fsdp": (z + NZ + 2 * side) % NZ})
            zx[side, step, sub] = copy_to(held, held, {"fsdp": (z + NZ + side) % NZ})

    def send_ya(step, sub):
        if step > 1:
            for side in sides:
                arrived(ya[side, step - 1, sub])
        pair = pl.ds(2 * sub, 2)
        for side in sides:
            source = wa.at[SLOT[-side * (step - 1)], pair]
            if step == 3 and side == sides[sub]:
                ya[side, 4, sub] = copy_to(
                    source, wa.at[SLOT[4], pair], chip(row_at(2 * side), x)
                )
            ya[side, step, sub] = copy_to(
                source, wa.at[SLOT[-side * step], pair], chip(row_at(side), x)
            )

    def row_chain():
        for entry in g_in:
            arrived(entry)
        wide = z_chain.shape[1]
        lane, line = iota((HEAD, wide), 1), iota((HEAD, wide), 0)
        chain = (lane == line + ROW * HEAD).astype(F32)
        for j in range(ROW):
            z_all[j] = cat(*split(chain), axis=1)
            p_all[j] = pack(chain[:, ROW * HEAD : (ROW + 1) * HEAD])
            chain = chain_step(g_row[j], chain) + (lane == line + j * HEAD).astype(F32)
        z_chain[...] = chain

    def send_g_col():
        total = pack(z_chain[...][:, ROW * HEAD : (ROW + 1) * HEAD])
        g_col[y] = total
        for d in FAR_FIRST:
            n = next(counter)
            conditional.append(
                [d, False, pltpu.make_async_remote_copy(
                    src_ref=g_col.at[y], dst_ref=g_col.at[y], send_sem=send.at[n], recv_sem=recv.at[n],
                    device_id=chip((y + d) % NY, x), device_id_type=MESH,
                )]
            )

            @pl.when(y + d < NY)
            def _(copy=conditional[-1][2]):
                copy.start()

    def column_chain():
        arrived_from_below(NY - 1)
        lane, line = iota((HEAD, NY * HEAD), 1), iota((HEAD, NY * HEAD), 0)
        chain = jnp.zeros((HEAD, NY * HEAD), F32)
        for q in range(NY - 1):
            longer = chain_step(g_col[q], chain) + (lane == line + q * HEAD).astype(F32)
            chain = jnp.where(q < y, longer, chain)
        z_row[...] = cat(*split(chain), axis=0)

    stages = prepare(
        r_ref, k_ref, a_ref, decay_ref, bonus_ref, y_ref, q_ref, h_ref, g_ref, coef_ref
    )

    def compute(steps=1):
        for _ in range(steps):
            next(stages, None)

    prev = copy_to(x_hbm.at[pl.ds(TOKENS - 16, 16)], prev_buf, at_seq((s + 1) % count))
    a_in = [copy_to(own_a, wa.at[0, x], chip(y, (x + d) % NX)) for d in (2, 1, 3)]
    send_yb(1)
    send_xb(0, 1)
    for load in loads:
        load.wait()
    compute()

    arrived(prev)
    own = x_ref[...].astype(F32)
    before = jnp.where(s == 0, 0.0, prev_buf[...].astype(F32)[15:16, :])
    shifted = jnp.where(iota((TOKENS, WIDTH), 0) == 0, before, pltpu.roll(own, 1, 0))
    mixed = own + (shifted - own) * blend_ref[...]
    even = cat(*[mixed[:, 128 * q : 128 * q + 64] for q in range(4)], axis=1).astype(BF16)
    odd = cat(*[mixed[:, 128 * q + 64 : 128 * q + 128] for q in range(4)], axis=1).astype(BF16)
    is_even = core == 0
    xg[z, core] = jnp.where(is_even, even, odd)
    x_send[...] = jnp.where(is_even, odd, even)
    mate_x = copy_to(x_send, xg.at[z, core], mate)
    send_zx(1, 0)
    for entry in a_in:
        arrived(entry)
    send_ya(1, 0)
    send_ya(1, 1)
    arrived(mate_x)
    send_zx(1, 1)
    send_yb(2)
    send_xb(1, 2)
    compute(7)
    send_zx(2, 0)
    send_ya(2, 0)
    send_zx(2, 1)
    send_ya(2, 1)
    send_yb(3)
    send_xb(3, 2)
    compute(4)
    g_in = []
    for d in FAR_FIRST:
        to = (place + d) % ROW
        g_in.append(copy_to(g_ref.at[to], g_row.at[place], at_seq(y * ROW + to)))
    g_row[place] = g_ref[place]
    send_zx(3, 0)
    send_ya(3, 0)
    send_zx(3, 1)
    send_ya(3, 1)
    for side, step in ((1, 3), (-1, 3), (1, 4)):
        arrived(yb[side, step])
    send_xb(5, 3)
    compute(100)
    row_chain()
    send_g_col()
    for entry in list(zx.values()) + list(ya.values()):
        arrived(entry)

    partial = []
    for half, weights in enumerate((wa, wb)):
        if half:
            for entry in waiting[:-1]:
                arrived(entry)
        total = jnp.zeros((2 * TOKENS, 256), F32)
        for slot, offset in enumerate(OFFSETS):
            total = total + dot(
                xg[row_at(offset)].reshape(2 * TOKENS, 256), weights[slot].reshape(256, 256)
            )
        p_send[half] = total.reshape(2, TOKENS, 256)
        partial.append(copy_to(p_send.at[half, 1 - core], p_recv.at[half], mate))
    values, doubled = [], []
    for half in range(2):
        arrived(partial[half])
        values.append((p_send[half, core] + p_recv[half]).astype(BF16))
        for h in range(HEADS // 2 * half, HEADS // 2 * (half + 1)):
            v = values[half][:, HEAD * (h % 4) : HEAD * (h % 4 + 1)]
            doubled.append(cat(v, v, axis=0))
            l_send[h] = pack(dot(h_ref[h], doubled[h]))
    value = cat(*values, axis=1)
    l_in = []
    for d in FAR_FIRST:
        to = (place + d) % ROW
        l_in.append(copy_to(l_send.at[to], l_row.at[place], at_seq(y * ROW + to)))
    l_row[place] = l_send[place]
    chain = z_chain[...][:, : ROW * HEAD]
    row_total = cat(*split(chain), axis=0)
    for entry in l_in:
        arrived(entry)
    lows = l_row[...].reshape(ROW * HEAD, 2 * HEAD)
    total = fold(dot(row_total, lows))
    t_send[...] = pack(total[:HEAD] + total[HEAD:])
    for d in FAR_FIRST:
        n = next(counter)
        conditional.append(
            [d, False, pltpu.make_async_remote_copy(
                src_ref=t_send, dst_ref=t_col.at[y], send_sem=send.at[n], recv_sem=recv.at[n],
                device_id=chip((y + d) % NY, x), device_id_type=MESH,
            )]
        )

        @pl.when(y + d < NY)
        def _(copy=conditional[-1][2]):
            copy.start()

    wide = ROW * HEAD
    span = z_all.shape[2] // 2
    from_row = []
    for j in range(ROW):
        both = cat(z_all[j, :, :wide], z_all[j, :, span : span + wide], axis=1)
        from_row.append(dot(both, cat(lows, lows, axis=0)))
    reads = [dot(y_ref[h], doubled[h]) for h in range(HEADS)]
    extra = coef_ref[...] * value.astype(F32)
    gate = gate_ref[...].astype(F32)

    column_chain()
    arrived_from_below()
    entering = fold(dot(z_row[...], t_col[...].reshape(NY * HEAD, 2 * HEAD)))
    entering = pack(entering[:HEAD] + entering[HEAD:])
    twice = cat(entering, entering, axis=0)
    entered = dot(p_all[...].reshape(ROW * HEAD, 2 * HEAD), twice)
    for j in range(ROW):
        s_send[j] = pack(fold(from_row[j] + entered[HEAD * j : HEAD * (j + 1)]))
    s_wait = []
    for d in FAR_FIRST:
        to = (place + d) % ROW
        s_wait.append(copy_to(s_send.at[to], s_in.at[place], at_seq(y * ROW + to)))
    s_in[place] = s_send[place]
    for entry in s_wait:
        arrived(entry)
    for h in range(HEADS):
        state = s_in[h]
        reads[h] = reads[h] + fold(dot(q_ref[h], cat(state, state, axis=0)))
    read = cat(*reads, axis=1)
    centre = read - head_sums(read) * (1.0 / HEAD)
    spread = head_sums(centre * centre) * (1.0 / HEAD)
    normed = centre * lax.rsqrt(spread + NORM_EPS) * scale_ref[...] + offset_ref[...]
    out_ref[...] = ((normed + extra) * gate).astype(BF16)

    finish()


COPIES = 128
SCRATCH = (
    pltpu.VMEM((TOKENS, WIDTH), BF16),
    pltpu.VMEM((TOKENS, WIDTH), BF16),
    pltpu.VMEM((TOKENS, WIDTH), BF16),
    pltpu.VMEM((TOKENS, WIDTH), BF16),
    pltpu.VMEM((TOKENS, WIDTH), F32),
    pltpu.VMEM((TOKENS, WIDTH), BF16),
    pltpu.VMEM((HEADS, TOKENS, 2 * TOKENS), BF16),
    pltpu.VMEM((HEADS, TOKENS, 2 * HEAD), BF16),
    pltpu.VMEM((HEADS, HEAD, 2 * TOKENS), BF16),
    pltpu.VMEM((HEADS, HEAD, 2 * HEAD), BF16),
    pltpu.VMEM((TOKENS, WIDTH), F32),
    pltpu.VMEM((16, WIDTH), BF16),
    pltpu.VMEM((TOKENS, 256), BF16),
    pltpu.VMEM((NZ, 2, TOKENS, 256), BF16),
    pltpu.VMEM((NY, NX, HEAD, 256), BF16),
    pltpu.VMEM((NY, NX, HEAD, 256), BF16),
    pltpu.VMEM((2, 2, TOKENS, 256), F32),
    pltpu.VMEM((2, TOKENS, 256), F32),
    pltpu.VMEM((ROW, HEAD, 2 * HEAD), BF16),
    pltpu.VMEM((NY, HEAD, 2 * HEAD), BF16),
    pltpu.VMEM((HEAD, 640), F32),
    pltpu.VMEM((ROW, HEAD, 2 * 640), BF16),
    pltpu.VMEM((ROW, HEAD, 2 * HEAD), BF16),
    pltpu.VMEM((2 * HEAD, NY * HEAD), BF16),
    pltpu.VMEM((HEADS, HEAD, 2 * HEAD), BF16),
    pltpu.VMEM((ROW, HEAD, 2 * HEAD), BF16),
    pltpu.VMEM((HEAD, 2 * HEAD), BF16),
    pltpu.VMEM((NY, HEAD, 2 * HEAD), BF16),
    pltpu.VMEM((ROW, HEAD, 2 * HEAD), BF16),
    pltpu.VMEM((HEADS, HEAD, 2 * HEAD), BF16),
    pltpu.SemaphoreType.DMA((COPIES,)),
    pltpu.SemaphoreType.DMA((COPIES,)),
    pltpu.SemaphoreType.DMA((8,)),
)


def shards(
    activation_entries,
    content_mapping_matrix,
    content_lagged_blend,
    acceptance_vectors,
    address_vectors_given,
    inline_adaptation_speed,
    memory_fading_factors,
    result_filter_given,
    extra_coordinate_factors,
    group_layernorm_scaling,
    group_layernorm_offset,
):
    vmem = pl.BlockSpec(memory_space=pltpu.VMEM)

    def row(vector):
        return vector.reshape(1, WIDTH)

    hbm = pl.BlockSpec(memory_space=pltpu.HBM)

    def pin(array):
        return pltpu.with_memory_space_constraint(array, pltpu.HBM)

    return pl.pallas_call(
        time_mix,
        out_shape=jax.ShapeDtypeStruct((TOKENS, WIDTH), BF16),
        in_specs=[hbm] * 7 + [vmem] * 4,
        out_specs=vmem,
        scratch_shapes=SCRATCH,
        compiler_params=pltpu.CompilerParams(
            collective_id=0, has_side_effects=True, vmem_limit_bytes=48 << 20
        ),
        name="time_mix",
    )(
        pin(activation_entries),
        pin(content_mapping_matrix),
        pin(acceptance_vectors),
        pin(address_vectors_given),
        pin(inline_adaptation_speed),
        pin(memory_fading_factors),
        pin(result_filter_given),
        pin(row(content_lagged_blend)),
        pin(row(extra_coordinate_factors)),
        pin(row(group_layernorm_scaling)),
        pin(row(group_layernorm_offset)),
    )


def solution(mesh):
    return jax.shard_map(
        shards,
        mesh=mesh,
        in_specs=(
            P("seq", "fsdp"),
            P("seq", "fsdp"),
            P("fsdp"),
            P("seq", "fsdp"),
            P("seq", "fsdp"),
            P("seq", "fsdp"),
            P("seq", "fsdp"),
            P("seq", "fsdp"),
            P("fsdp"),
            P("fsdp"),
            P("fsdp"),
        ),
        out_specs=P("seq", "fsdp"),
        check_vma=False,
    )
```

```python
import functools

import jax
import jax.numpy as jnp
from jax import lax
from jax.experimental import pallas as pl
from jax.experimental.pallas import tpu as pltpu
from jax.sharding import PartitionSpec as P

MESH = pl.DeviceIdType.MESH
F32 = jnp.float32
BF16 = jnp.bfloat16
HEAD = 64
HEADS = 8
TOKENS = 128
WIDTH = HEAD * HEADS
NX, NY, NZ = 4, 8, 8
ROW = 2 * NX
OFFSETS = (0, -1, 1, -2, 2, -3, 3, 4)
SLOT = {offset: n for n, offset in enumerate(OFFSETS)} | {-4: 7}
FAR_FIRST = (4, 3, 5, 2, 6, 1, 7)
NORM_EPS = 0.00064
UNIT_EPS = 1e-05


def split(x):
    high = x.astype(BF16)
    return high, (x - high.astype(F32)).astype(BF16)


def cat(*parts, axis):
    return jnp.concatenate(parts, axis=axis)


def dot(a, b):
    return jnp.dot(a, b, preferred_element_type=F32)


def dot_nt(a, b):
    return lax.dot_general(a, b, (((1,), (1,)), ((), ())), preferred_element_type=F32)


def wide_left(high, low):
    return cat(high, low, high, axis=1)


def wide_right(high, low):
    return cat(high, high, low, axis=0)


def iota(shape, dim):
    return lax.broadcasted_iota(jnp.int32, shape, dim)


def head_sums(x):
    ones = ((iota((256, 256), 0) // HEAD) == (iota((256, 256), 1) // HEAD)).astype(BF16)
    high, low = split(x)
    sums = dot(cat(high[:, :256], high[:, 256:], axis=0), ones) + dot(
        cat(low[:, :256], low[:, 256:], axis=0), ones
    )
    return cat(sums[:TOKENS], sums[TOKENS:], axis=1)


def shift_rows(x, steps, fill):
    rows = iota(x.shape, 0)
    return jnp.where(rows < steps, fill, pltpu.roll(x, steps, 0))


def prepare(r_ref, k_ref, a_ref, w_ref, bonus_ref, y_ref, q_ref, h_ref, g_ref, coef_ref):
    r = r_ref[...].astype(F32)
    k = k_ref[...].astype(F32)
    a = a_ref[...].astype(F32)
    unit = k * lax.rsqrt(head_sums(k * k) + UNIT_EPS)
    coef_ref[...] = head_sums(r * k * bonus_ref[...])
    cumul = w_ref[...]
    for level in range(7):
        cumul = cumul * shift_rows(cumul, 1 << level, 1.0)
    yield
    before = shift_rows(cumul, 1, 1.0)
    inverse = 1.0 / cumul
    end = cumul[TOKENS - 1 :, :]
    erase = -unit * before
    write = unit * a * inverse
    key = k * inverse
    rec = r * cumul
    erase_h, erase_l = split(erase)
    write_h, write_l = split(write)
    key_h, key_l = split(key)
    rec_h, rec_l = split(rec)
    write_end = write * end
    key_end = key * end
    rows, cols = iota((TOKENS, TOKENS), 0), iota((TOKENS, TOKENS), 1)
    strict, inclusive = rows > cols, rows >= cols
    differ = rows ^ cols
    eye = (rows == cols).astype(F32)
    small_eye = iota((HEAD, HEAD), 0) == iota((HEAD, HEAD), 1)

    grams, solves = [], []
    for h in range(HEADS):
        at = slice(HEAD * h, HEAD * (h + 1))
        left = wide_left(
            cat(erase_h[:, at], rec_h[:, at], axis=0), cat(erase_l[:, at], rec_l[:, at], axis=0)
        )
        high = cat(write_h[:, at], key_h[:, at], axis=0)
        low = cat(write_l[:, at], key_l[:, at], axis=0)
        grams.append(dot_nt(left, cat(high, high, low, axis=1)))
        if h == HEADS // 2 - 1:
            yield
    systems = [jnp.where(strict, gram[:TOKENS, :TOKENS], 0.0) for gram in grams]
    halves = [split(system) for system in systems]
    for h in range(HEADS):
        solves.append(eye + jnp.where(differ == 1, systems[h], 0.0))
    yield
    for level in range(1, 7):
        mask = (differ >> level) == 1
        for h in range(HEADS):
            rough = solves[h].astype(BF16)
            part = jnp.where(mask, halves[h][0], jnp.zeros_like(halves[h][0]))
            solves[h] = solves[h] + dot(rough, dot(part, rough).astype(BF16))
        yield
    for h in range(HEADS):
        high, low = split(solves[h])
        left_over = eye - solves[h] + dot(wide_left(*halves[h]), wide_right(high, low))
        solves[h] = solves[h] + dot(high, left_over.astype(BF16))
    yield
    inverses = [wide_left(*split(solve)) for solve in solves]
    mixes = []
    for pair in range(HEADS // 2):
        wide = slice(2 * HEAD * pair, 2 * HEAD * (pair + 1))
        write_t = write_end[:, wide].T
        for half in range(2):
            h = 2 * pair + half
            at = slice(HEAD * h, HEAD * (h + 1))
            keyed = dot(inverses[h], wide_right(erase_h[:, at], erase_l[:, at]))
            read_write = jnp.where(inclusive, grams[h][TOKENS:, :TOKENS], 0.0)
            mine = slice(HEAD * half, HEAD * (half + 1))
            mixes.append(wide_left(*split(cat(read_write, write_t[mine], axis=0))))
            out = dot(mixes[h], wide_right(*split(keyed)))
            q_ref[h] = cat(*split(rec[:, at] + out[:TOKENS]), axis=1)
            diagonal = jnp.where(small_eye, end[:, at], 0.0)
            g_ref[h] = cat(*split(diagonal + out[TOKENS:]), axis=1)
        if pair % 2:
            yield
    for pair in range(HEADS // 2):
        wide = slice(2 * HEAD * pair, 2 * HEAD * (pair + 1))
        key_t = key_end[:, wide].T
        for half in range(2):
            h = 2 * pair + half
            gram = grams[h]
            erase_key = jnp.where(strict, gram[:TOKENS, TOKENS:], 0.0)
            read_key = jnp.where(inclusive, gram[TOKENS:, TOKENS:], 0.0)
            valued = dot(inverses[h], wide_right(*split(erase_key)))
            out = dot(mixes[h], wide_right(*split(valued)))
            mine = slice(HEAD * half, HEAD * (half + 1))
            y_ref[h] = cat(*split(read_key + out[:TOKENS]), axis=1)
            h_ref[h] = cat(*split(key_t[mine] + out[TOKENS:]), axis=1)
        if pair % 2:
            yield


def chain_step(g, z):
    high, low = split(z)
    return dot(cat(g, g[:, :HEAD], axis=1), wide_right(high, low))


def fold(x):
    return x[:, :HEAD] + x[:, HEAD:]


def pack(x):
    return cat(*split(x), axis=1)


def time_mix(
    x_hbm, w_ref, r_hbm, k_hbm, a_hbm, decay_hbm, gate_hbm, blend_ref, bonus_ref, scale_ref, offset_ref,
    out_ref,
    x_ref, r_ref, k_ref, a_ref, decay_ref, gate_ref,
    y_ref, q_ref, h_ref, g_ref, coef_ref,
    prev_buf, x_send, xg, wa, wb, p_send, p_recv,
    g_row, g_col, z_chain, z_all, p_all, z_row,
    l_send, l_row, t_send, t_col, s_send, s_in,
    send, recv, local,
):
    s, z = lax.axis_index("seq"), lax.axis_index("fsdp")
    count = NX * NY * 2
    core, x, y, place = s % 2, (s // 2) % NX, s // ROW, s % ROW
    counter = iter(range(10**6))
    waiting, conditional = [], []

    def at_seq(index):
        return {"seq": index}

    def chip(yy, xx):
        return at_seq((yy * NX + xx) * 2 + core)

    def copy_to(source, target, device):
        n = next(counter)
        copy = pltpu.make_async_remote_copy(
            src_ref=source, dst_ref=target, send_sem=send.at[n], recv_sem=recv.at[n],
            device_id=device, device_id_type=MESH,
        )
        copy.start()
        entry = [copy, False]
        waiting.append(entry)
        return entry

    def arrived(entry):
        if not entry[1]:
            entry[1] = True
            entry[0].wait_recv()

    def arrived_from_below(number=None):
        for entry in conditional[:number]:
            if not entry[1]:
                entry[1] = True

                @pl.when(y >= entry[0])
                def _(copy=entry[2]):
                    copy.wait_recv()

    def finish():
        for entry in waiting:
            entry[0].wait_send()
        for d, _, copy in conditional:

            @pl.when(y + d < NY)
            def _(copy=copy):
                copy.wait_send()

    mate = at_seq(s + 1 - 2 * core)
    sides = (1, -1)
    barrier = pltpu.get_barrier_semaphore()
    partners = [chip(y, (x + d) % NX) for d in range(1, NX)]
    partners += [chip((y + NY + side) % NY, x) for side in sides]
    partners += [{"fsdp": (z + NZ + side) % NZ} for side in sides]
    partners += [mate, at_seq((s + count - 1 + 2 * core) % count)]
    for partner in partners:
        pl.semaphore_signal(barrier, inc=1, device_id=partner, device_id_type=MESH)
    own_a, own_b = w_ref.at[:, pl.ds(0, 256)], w_ref.at[:, pl.ds(256, 256)]
    loads = [
        pltpu.make_async_copy(source, target, local.at[n])
        for n, (source, target) in enumerate(
            (
                (x_hbm, x_ref),
                (own_a, wa.at[0, x]),
                (own_b, wb.at[0, x]),
                (r_hbm, r_ref),
                (k_hbm, k_ref),
                (a_hbm, a_ref),
                (decay_hbm, decay_ref),
                (gate_hbm, gate_ref),
            )
        )
    ]
    for load in loads:
        load.start()
    for d in range(NY):
        t_col[d] = jnp.zeros((HEAD, 2 * HEAD), BF16)
    pl.semaphore_wait(barrier, len(partners))

    yb, ya, zx = {}, {}, {}

    def row_at(offset):
        return (y + offset + NY) % NY

    def send_yb(step):
        if step > 1:
            for side in sides:
                arrived(yb[side, step - 1])
        for side in sides:
            source = own_b if step == 1 else wb.at[SLOT[-side * (step - 1)], x]
            yb[side, step] = copy_to(source, wb.at[SLOT[-side * step], x], chip(row_at(side), x))
            if step == 3 and side > 0:
                yb[side, 4] = copy_to(
                    wb.at[SLOT[-2 * side], x], wb.at[SLOT[4], x], chip(row_at(2 * side), x)
                )

    def send_xb(first, number):
        part = wb.at[pl.ds(first, number), x]
        for d in (2, 1, 3):
            if first == 0:
                copy_to(own_b, wb.at[0, x], chip(y, (x + d) % NX))
            else:
                copy_to(part, part, chip(y, (x + d) % NX))

    def send_zx(step, sub):
        part = core if sub == 0 else 1 - core
        if step > 1:
            for side in sides:
                arrived(zx[side, step - 1, sub])
        for side in sides:
            block = (z + NZ - side * (step - 1)) % NZ
            held = xg.at[block, part]
            if step == 3 and side == sides[sub]:
                zx[side, 4, sub] = copy_to(held, held, {"fsdp": (z + NZ + 2 * side) % NZ})
            zx[side, step, sub] = copy_to(held, held, {"fsdp": (z + NZ + side) % NZ})

    def send_ya(step, sub):
        if step > 1:
            for side in sides:
                arrived(ya[side, step - 1, sub])
        pair = pl.ds(2 * sub, 2)
        for side in sides:
            source = wa.at[SLOT[-side * (step - 1)], pair]
            if step == 3 and side == sides[sub]:
                ya[side, 4, sub] = copy_to(
                    source, wa.at[SLOT[4], pair], chip(row_at(2 * side), x)
                )
            ya[side, step, sub] = copy_to(
                source, wa.at[SLOT[-side * step], pair], chip(row_at(side), x)
            )

    def row_chain():
        for entry in g_in:
            arrived(entry)
        wide = z_chain.shape[1]
        lane, line = iota((HEAD, wide), 1), iota((HEAD, wide), 0)
        chain = (lane == line + ROW * HEAD).astype(F32)
        for j in range(ROW):
            z_all[j] = cat(*split(chain), axis=1)
            p_all[j] = pack(chain[:, ROW * HEAD : (ROW + 1) * HEAD])
            chain = chain_step(g_row[j], chain) + (lane == line + j * HEAD).astype(F32)
        z_chain[...] = chain

    def send_g_col():
        total = pack(z_chain[...][:, ROW * HEAD : (ROW + 1) * HEAD])
        g_col[y] = total
        for d in FAR_FIRST:
            n = next(counter)
            conditional.append(
                [d, False, pltpu.make_async_remote_copy(
                    src_ref=g_col.at[y], dst_ref=g_col.at[y], send_sem=send.at[n], recv_sem=recv.at[n],
                    device_id=chip((y + d) % NY, x), device_id_type=MESH,
                )]
            )

            @pl.when(y + d < NY)
            def _(copy=conditional[-1][2]):
                copy.start()

    def column_chain():
        arrived_from_below(NY - 1)
        lane, line = iota((HEAD, NY * HEAD), 1), iota((HEAD, NY * HEAD), 0)
        chain = jnp.zeros((HEAD, NY * HEAD), F32)
        for q in range(NY - 1):
            longer = chain_step(g_col[q], chain) + (lane == line + q * HEAD).astype(F32)
            chain = jnp.where(q < y, longer, chain)
        z_row[...] = cat(*split(chain), axis=0)

    stages = prepare(
        r_ref, k_ref, a_ref, decay_ref, bonus_ref, y_ref, q_ref, h_ref, g_ref, coef_ref
    )

    def compute(steps=1):
        for _ in range(steps):
            next(stages, None)

    prev = copy_to(x_hbm.at[pl.ds(TOKENS - 16, 16)], prev_buf, at_seq((s + 1) % count))
    a_in = [copy_to(own_a, wa.at[0, x], chip(y, (x + d) % NX)) for d in (2, 1, 3)]
    send_yb(1)
    send_xb(0, 1)
    for load in loads:
        load.wait()

    arrived(prev)
    own = x_ref[...].astype(F32)
    before = jnp.where(s == 0, 0.0, prev_buf[...].astype(F32)[15:16, :])
    shifted = jnp.where(iota((TOKENS, WIDTH), 0) == 0, before, pltpu.roll(own, 1, 0))
    mixed = own + (shifted - own) * blend_ref[...]
    even = cat(*[mixed[:, 128 * q : 128 * q + 64] for q in range(4)], axis=1).astype(BF16)
    odd = cat(*[mixed[:, 128 * q + 64 : 128 * q + 128] for q in range(4)], axis=1).astype(BF16)
    is_even = core == 0
    xg[z, core] = jnp.where(is_even, even, odd)
    x_send[...] = jnp.where(is_even, odd, even)
    mate_x = copy_to(x_send, xg.at[z, core], mate)
    send_zx(1, 0)
    for entry in a_in:
        arrived(entry)
    send_ya(1, 0)
    send_ya(1, 1)
    arrived(mate_x)
    send_zx(1, 1)
    send_yb(2)
    send_xb(1, 2)
    compute(8)
    send_zx(2, 0)
    send_ya(2, 0)
    send_zx(2, 1)
    send_ya(2, 1)
    send_yb(3)
    send_xb(3, 2)
    compute(4)
    g_in = []
    for d in FAR_FIRST:
        to = (place + d) % ROW
        g_in.append(copy_to(g_ref.at[to], g_row.at[place], at_seq(y * ROW + to)))
    g_row[place] = g_ref[place]
    send_zx(3, 0)
    send_ya(3, 0)
    send_zx(3, 1)
    send_ya(3, 1)
    for side, step in ((1, 3), (-1, 3), (1, 4)):
        arrived(yb[side, step])
    send_xb(5, 3)
    compute(100)
    row_chain()
    send_g_col()
    for entry in list(zx.values()) + list(ya.values()):
        arrived(entry)

    partial = []
    for half, weights in enumerate((wa, wb)):
        if half:
            for entry in waiting[:-1]:
                arrived(entry)
        total = jnp.zeros((2 * TOKENS, 256), F32)
        for slot, offset in enumerate(OFFSETS):
            total = total + dot(
                xg[row_at(offset)].reshape(2 * TOKENS, 256), weights[slot].reshape(256, 256)
            )
        p_send[half] = total.reshape(2, TOKENS, 256)
        partial.append(copy_to(p_send.at[half, 1 - core], p_recv.at[half], mate))
    values, doubled = [], []
    for half in range(2):
        arrived(partial[half])
        values.append((p_send[half, core] + p_recv[half]).astype(BF16))
        for h in range(HEADS // 2 * half, HEADS // 2 * (half + 1)):
            v = values[half][:, HEAD * (h % 4) : HEAD * (h % 4 + 1)]
            doubled.append(cat(v, v, axis=0))
            l_send[h] = pack(dot(h_ref[h], doubled[h]))
    value = cat(*values, axis=1)
    l_in = []
    for d in FAR_FIRST:
        to = (place + d) % ROW
        l_in.append(copy_to(l_send.at[to], l_row.at[place], at_seq(y * ROW + to)))
    l_row[place] = l_send[place]
    chain = z_chain[...][:, : ROW * HEAD]
    row_total = cat(*split(chain), axis=0)
    for entry in l_in:
        arrived(entry)
    lows = l_row[...].reshape(ROW * HEAD, 2 * HEAD)
    total = fold(dot(row_total, lows))
    t_send[...] = pack(total[:HEAD] + total[HEAD:])
    for d in FAR_FIRST:
        n = next(counter)
        conditional.append(
            [d, False, pltpu.make_async_remote_copy(
                src_ref=t_send, dst_ref=t_col.at[y], send_sem=send.at[n], recv_sem=recv.at[n],
                device_id=chip((y + d) % NY, x), device_id_type=MESH,
            )]
        )

        @pl.when(y + d < NY)
        def _(copy=conditional[-1][2]):
            copy.start()

    wide = ROW * HEAD
    span = z_all.shape[2] // 2
    from_row = []
    for j in range(ROW):
        both = cat(z_all[j, :, :wide], z_all[j, :, span : span + wide], axis=1)
        from_row.append(dot(both, cat(lows, lows, axis=0)))
    reads = [dot(y_ref[h], doubled[h]) for h in range(HEADS)]
    extra = coef_ref[...] * value.astype(F32)
    gate = gate_ref[...].astype(F32)

    column_chain()
    arrived_from_below()
    entering = fold(dot(z_row[...], t_col[...].reshape(NY * HEAD, 2 * HEAD)))
    entering = pack(entering[:HEAD] + entering[HEAD:])
    twice = cat(entering, entering, axis=0)
    entered = dot(p_all[...].reshape(ROW * HEAD, 2 * HEAD), twice)
    for j in range(ROW):
        s_send[j] = pack(fold(from_row[j] + entered[HEAD * j : HEAD * (j + 1)]))
    s_wait = []
    for d in FAR_FIRST:
        to = (place + d) % ROW
        s_wait.append(copy_to(s_send.at[to], s_in.at[place], at_seq(y * ROW + to)))
    s_in[place] = s_send[place]
    for entry in s_wait:
        arrived(entry)
    for h in range(HEADS):
        state = s_in[h]
        reads[h] = reads[h] + fold(dot(q_ref[h], cat(state, state, axis=0)))
    read = cat(*reads, axis=1)
    centre = read - head_sums(read) * (1.0 / HEAD)
    spread = head_sums(centre * centre) * (1.0 / HEAD)
    normed = centre * lax.rsqrt(spread + NORM_EPS) * scale_ref[...] + offset_ref[...]
    out_ref[...] = ((normed + extra) * gate).astype(BF16)

    finish()


COPIES = 128
SCRATCH = (
    pltpu.VMEM((TOKENS, WIDTH), BF16),
    pltpu.VMEM((TOKENS, WIDTH), BF16),
    pltpu.VMEM((TOKENS, WIDTH), BF16),
    pltpu.VMEM((TOKENS, WIDTH), BF16),
    pltpu.VMEM((TOKENS, WIDTH), F32),
    pltpu.VMEM((TOKENS, WIDTH), BF16),
    pltpu.VMEM((HEADS, TOKENS, 2 * TOKENS), BF16),
    pltpu.VMEM((HEADS, TOKENS, 2 * HEAD), BF16),
    pltpu.VMEM((HEADS, HEAD, 2 * TOKENS), BF16),
    pltpu.VMEM((HEADS, HEAD, 2 * HEAD), BF16),
    pltpu.VMEM((TOKENS, WIDTH), F32),
    pltpu.VMEM((16, WIDTH), BF16),
    pltpu.VMEM((TOKENS, 256), BF16),
    pltpu.VMEM((NZ, 2, TOKENS, 256), BF16),
    pltpu.VMEM((NY, NX, HEAD, 256), BF16),
    pltpu.VMEM((NY, NX, HEAD, 256), BF16),
    pltpu.VMEM((2, 2, TOKENS, 256), F32),
    pltpu.VMEM((2, TOKENS, 256), F32),
    pltpu.VMEM((ROW, HEAD, 2 * HEAD), BF16),
    pltpu.VMEM((NY, HEAD, 2 * HEAD), BF16),
    pltpu.VMEM((HEAD, 640), F32),
    pltpu.VMEM((ROW, HEAD, 2 * 640), BF16),
    pltpu.VMEM((ROW, HEAD, 2 * HEAD), BF16),
    pltpu.VMEM((2 * HEAD, NY * HEAD), BF16),
    pltpu.VMEM((HEADS, HEAD, 2 * HEAD), BF16),
    pltpu.VMEM((ROW, HEAD, 2 * HEAD), BF16),
    pltpu.VMEM((HEAD, 2 * HEAD), BF16),
    pltpu.VMEM((NY, HEAD, 2 * HEAD), BF16),
    pltpu.VMEM((ROW, HEAD, 2 * HEAD), BF16),
    pltpu.VMEM((HEADS, HEAD, 2 * HEAD), BF16),
    pltpu.SemaphoreType.DMA((COPIES,)),
    pltpu.SemaphoreType.DMA((COPIES,)),
    pltpu.SemaphoreType.DMA((8,)),
)


def shards(
    activation_entries,
    content_mapping_matrix,
    content_lagged_blend,
    acceptance_vectors,
    address_vectors_given,
    inline_adaptation_speed,
    memory_fading_factors,
    result_filter_given,
    extra_coordinate_factors,
    group_layernorm_scaling,
    group_layernorm_offset,
):
    vmem = pl.BlockSpec(memory_space=pltpu.VMEM)

    def row(vector):
        return vector.reshape(1, WIDTH)

    hbm = pl.BlockSpec(memory_space=pltpu.HBM)

    def pin(array):
        return pltpu.with_memory_space_constraint(array, pltpu.HBM)

    return pl.pallas_call(
        time_mix,
        out_shape=jax.ShapeDtypeStruct((TOKENS, WIDTH), BF16),
        in_specs=[hbm] * 7 + [vmem] * 4,
        out_specs=vmem,
        scratch_shapes=SCRATCH,
        compiler_params=pltpu.CompilerParams(
            collective_id=0, has_side_effects=True, vmem_limit_bytes=48 << 20
        ),
        name="time_mix",
    )(
        pin(activation_entries),
        pin(content_mapping_matrix),
        pin(acceptance_vectors),
        pin(address_vectors_given),
        pin(inline_adaptation_speed),
        pin(memory_fading_factors),
        pin(result_filter_given),
        pin(row(content_lagged_blend)),
        pin(row(extra_coordinate_factors)),
        pin(row(group_layernorm_scaling)),
        pin(row(group_layernorm_offset)),
    )


def solution(mesh):
    return jax.shard_map(
        shards,
        mesh=mesh,
        in_specs=(
            P("seq", "fsdp"),
            P("seq", "fsdp"),
            P("fsdp"),
            P("seq", "fsdp"),
            P("seq", "fsdp"),
            P("seq", "fsdp"),
            P("seq", "fsdp"),
            P("seq", "fsdp"),
            P("fsdp"),
            P("fsdp"),
            P("fsdp"),
        ),
        out_specs=P("seq", "fsdp"),
        check_vma=False,
    )
```

```python
import functools

import jax
import jax.numpy as jnp
from jax import lax
from jax.experimental import pallas as pl
from jax.experimental.pallas import tpu as pltpu
from jax.sharding import PartitionSpec as P

MESH = pl.DeviceIdType.MESH
F32 = jnp.float32
BF16 = jnp.bfloat16
HEAD = 64
HEADS = 8
TOKENS = 128
WIDTH = HEAD * HEADS
NX, NY, NZ = 4, 8, 8
ROW = 2 * NX
OFFSETS = (0, -1, 1, -2, 2, -3, 3, 4)
SLOT = {offset: n for n, offset in enumerate(OFFSETS)} | {-4: 7}
FAR_FIRST = (4, 3, 5, 2, 6, 1, 7)
NORM_EPS = 0.00064
UNIT_EPS = 1e-05


def split(x):
    high = x.astype(BF16)
    return high, (x - high.astype(F32)).astype(BF16)


def cat(*parts, axis):
    return jnp.concatenate(parts, axis=axis)


def dot(a, b):
    return jnp.dot(a, b, preferred_element_type=F32)


def dot_nt(a, b):
    return lax.dot_general(a, b, (((1,), (1,)), ((), ())), preferred_element_type=F32)


def wide_left(high, low):
    return cat(high, low, high, axis=1)


def wide_right(high, low):
    return cat(high, high, low, axis=0)


def iota(shape, dim):
    return lax.broadcasted_iota(jnp.int32, shape, dim)


def head_sums(x):
    ones = ((iota((256, 256), 0) // HEAD) == (iota((256, 256), 1) // HEAD)).astype(BF16)
    high, low = split(x)
    sums = dot(cat(high[:, :256], high[:, 256:], axis=0), ones) + dot(
        cat(low[:, :256], low[:, 256:], axis=0), ones
    )
    return cat(sums[:TOKENS], sums[TOKENS:], axis=1)


def shift_rows(x, steps, fill):
    rows = iota(x.shape, 0)
    return jnp.where(rows < steps, fill, pltpu.roll(x, steps, 0))


def prepare(r_ref, k_ref, a_ref, w_ref, bonus_ref, y_ref, q_ref, h_ref, g_ref, coef_ref):
    r = r_ref[...].astype(F32)
    k = k_ref[...].astype(F32)
    a = a_ref[...].astype(F32)
    unit = k * lax.rsqrt(head_sums(k * k) + UNIT_EPS)
    coef_ref[...] = head_sums(r * k * bonus_ref[...])
    cumul = w_ref[...]
    for level in range(7):
        cumul = cumul * shift_rows(cumul, 1 << level, 1.0)
    yield
    before = shift_rows(cumul, 1, 1.0)
    inverse = 1.0 / cumul
    end = cumul[TOKENS - 1 :, :]
    erase = -unit * before
    write = unit * a * inverse
    key = k * inverse
    rec = r * cumul
    erase_h, erase_l = split(erase)
    write_h, write_l = split(write)
    key_h, key_l = split(key)
    rec_h, rec_l = split(rec)
    write_end = write * end
    key_end = key * end
    rows, cols = iota((TOKENS, TOKENS), 0), iota((TOKENS, TOKENS), 1)
    strict, inclusive = rows > cols, rows >= cols
    differ = rows ^ cols
    eye = (rows == cols).astype(F32)
    small_eye = iota((HEAD, HEAD), 0) == iota((HEAD, HEAD), 1)

    grams, solves = [], []
    for h in range(HEADS):
        at = slice(HEAD * h, HEAD * (h + 1))
        left = wide_left(
            cat(erase_h[:, at], rec_h[:, at], axis=0), cat(erase_l[:, at], rec_l[:, at], axis=0)
        )
        high = cat(write_h[:, at], key_h[:, at], axis=0)
        low = cat(write_l[:, at], key_l[:, at], axis=0)
        grams.append(dot_nt(left, cat(high, high, low, axis=1)))
        if h == HEADS // 2 - 1:
            yield
    systems = [jnp.where(strict, gram[:TOKENS, :TOKENS], 0.0) for gram in grams]
    halves = [split(system) for system in systems]
    for h in range(HEADS):
        solves.append(eye + jnp.where(differ == 1, systems[h], 0.0))
    yield
    for level in range(1, 7):
        mask = (differ >> level) == 1
        for h in range(HEADS):
            rough = solves[h].astype(BF16)
            part = jnp.where(mask, halves[h][0], jnp.zeros_like(halves[h][0]))
            solves[h] = solves[h] + dot(rough, dot(part, rough).astype(BF16))
        yield
    for h in range(HEADS):
        high, low = split(solves[h])
        left_over = eye - solves[h] + dot(wide_left(*halves[h]), wide_right(high, low))
        solves[h] = solves[h] + dot(high, left_over.astype(BF16))
    yield
    inverses = [wide_left(*split(solve)) for solve in solves]
    mixes = []
    for pair in range(HEADS // 2):
        wide = slice(2 * HEAD * pair, 2 * HEAD * (pair + 1))
        write_t = write_end[:, wide].T
        for half in range(2):
            h = 2 * pair + half
            at = slice(HEAD * h, HEAD * (h + 1))
            keyed = dot(inverses[h], wide_right(erase_h[:, at], erase_l[:, at]))
            read_write = jnp.where(inclusive, grams[h][TOKENS:, :TOKENS], 0.0)
            mine = slice(HEAD * half, HEAD * (half + 1))
            mixes.append(wide_left(*split(cat(read_write, write_t[mine], axis=0))))
            out = dot(mixes[h], wide_right(*split(keyed)))
            q_ref[h] = cat(*split(rec[:, at] + out[:TOKENS]), axis=1)
            diagonal = jnp.where(small_eye, end[:, at], 0.0)
            g_ref[h] = cat(*split(diagonal + out[TOKENS:]), axis=1)
        if pair % 2:
            yield
    for pair in range(HEADS // 2):
        wide = slice(2 * HEAD * pair, 2 * HEAD * (pair + 1))
        key_t = key_end[:, wide].T
        for half in range(2):
            h = 2 * pair + half
            gram = grams[h]
            erase_key = jnp.where(strict, gram[:TOKENS, TOKENS:], 0.0)
            read_key = jnp.where(inclusive, gram[TOKENS:, TOKENS:], 0.0)
            valued = dot(inverses[h], wide_right(*split(erase_key)))
            out = dot(mixes[h], wide_right(*split(valued)))
            mine = slice(HEAD * half, HEAD * (half + 1))
            y_ref[h] = cat(*split(read_key + out[:TOKENS]), axis=1)
            h_ref[h] = cat(*split(key_t[mine] + out[TOKENS:]), axis=1)
        if pair % 2:
            yield


def chain_step(g, z):
    high, low = split(z)
    return dot(cat(g, g[:, :HEAD], axis=1), wide_right(high, low))


def fold(x):
    return x[:, :HEAD] + x[:, HEAD:]


def pack(x):
    return cat(*split(x), axis=1)


def time_mix(
    x_hbm, w_ref, r_hbm, k_hbm, a_hbm, decay_hbm, gate_hbm, blend_ref, bonus_ref, scale_ref, offset_ref,
    out_ref,
    x_ref, r_ref, k_ref, a_ref, decay_ref, gate_ref,
    y_ref, q_ref, h_ref, g_ref, coef_ref,
    prev_buf, x_send, xg, wa, wb, p_send, p_recv,
    g_row, g_col, z_chain, z_all, p_all, z_row,
    l_send, l_row, t_send, t_col, s_send, s_in,
    send, recv, local,
):
    s, z = lax.axis_index("seq"), lax.axis_index("fsdp")
    count = NX * NY * 2
    core, x, y, place = s % 2, (s // 2) % NX, s // ROW, s % ROW
    counter = iter(range(10**6))
    waiting, conditional = [], []

    def at_seq(index):
        return {"seq": index}

    def chip(yy, xx):
        return at_seq((yy * NX + xx) * 2 + core)

    def copy_to(source, target, device):
        n = next(counter)
        copy = pltpu.make_async_remote_copy(
            src_ref=source, dst_ref=target, send_sem=send.at[n], recv_sem=recv.at[n],
            device_id=device, device_id_type=MESH,
        )
        copy.start()
        entry = [copy, False]
        waiting.append(entry)
        return entry

    def arrived(entry):
        if not entry[1]:
            entry[1] = True
            entry[0].wait_recv()

    def arrived_from_below(number=None):
        for entry in conditional[:number]:
            if not entry[1]:
                entry[1] = True

                @pl.when(y >= entry[0])
                def _(copy=entry[2]):
                    copy.wait_recv()

    def finish():
        for entry in waiting:
            entry[0].wait_send()
        for d, _, copy in conditional:

            @pl.when(y + d < NY)
            def _(copy=copy):
                copy.wait_send()

    mate = at_seq(s + 1 - 2 * core)
    sides = (1, -1)
    barrier = pltpu.get_barrier_semaphore()
    partners = [chip(y, (x + d) % NX) for d in range(1, NX)]
    partners += [chip((y + NY + side) % NY, x) for side in sides]
    partners += [{"fsdp": (z + NZ + side) % NZ} for side in sides]
    partners += [mate, at_seq((s + count - 1 + 2 * core) % count)]
    for partner in partners:
        pl.semaphore_signal(barrier, inc=1, device_id=partner, device_id_type=MESH)
    own_a, own_b = w_ref.at[:, pl.ds(0, 256)], w_ref.at[:, pl.ds(256, 256)]
    loads = [
        pltpu.make_async_copy(source, target, local.at[n])
        for n, (source, target) in enumerate(
            (
                (x_hbm, x_ref),
                (own_a, wa.at[0, x]),
                (own_b, wb.at[0, x]),
                (r_hbm, r_ref),
                (k_hbm, k_ref),
                (a_hbm, a_ref),
                (decay_hbm, decay_ref),
                (gate_hbm, gate_ref),
            )
        )
    ]
    for load in loads:
        load.start()
    for d in range(NY):
        t_col[d] = jnp.zeros((HEAD, 2 * HEAD), BF16)
    pl.semaphore_wait(barrier, len(partners))

    yb, ya, zx = {}, {}, {}

    def row_at(offset):
        return (y + offset + NY) % NY

    def send_yb(step):
        if step > 1:
            for side in sides:
                arrived(yb[side, step - 1])
        for side in sides:
            source = own_b if step == 1 else wb.at[SLOT[-side * (step - 1)], x]
            yb[side, step] = copy_to(source, wb.at[SLOT[-side * step], x], chip(row_at(side), x))
            if step == 3 and side > 0:
                yb[side, 4] = copy_to(
                    wb.at[SLOT[-2 * side], x], wb.at[SLOT[4], x], chip(row_at(2 * side), x)
                )

    def send_xb(first, number):
        part = wb.at[pl.ds(first, number), x]
        for d in (2, 1, 3):
            if first == 0:
                copy_to(own_b, wb.at[0, x], chip(y, (x + d) % NX))
            else:
                copy_to(part, part, chip(y, (x + d) % NX))

    def send_zx(step, sub):
        part = core if sub == 0 else 1 - core
        if step > 1:
            for side in sides:
                arrived(zx[side, step - 1, sub])
        for side in sides:
            block = (z + NZ - side * (step - 1)) % NZ
            held = xg.at[block, part]
            if step == 3 and side == sides[sub]:
                zx[side, 4, sub] = copy_to(held, held, {"fsdp": (z + NZ + 2 * side) % NZ})
            zx[side, step, sub] = copy_to(held, held, {"fsdp": (z + NZ + side) % NZ})

    def send_ya(step, sub):
        if step > 1:
            for side in sides:
                arrived(ya[side, step - 1, sub])
        pair = pl.ds(2 * sub, 2)
        for side in sides:
            source = wa.at[SLOT[-side * (step - 1)], pair]
            if step == 3 and side == sides[sub]:
                ya[side, 4, sub] = copy_to(
                    source, wa.at[SLOT[4], pair], chip(row_at(2 * side), x)
                )
            ya[side, step, sub] = copy_to(
                source, wa.at[SLOT[-side * step], pair], chip(row_at(side), x)
            )

    def row_chain():
        for entry in g_in:
            arrived(entry)
        wide = z_chain.shape[1]
        lane, line = iota((HEAD, wide), 1), iota((HEAD, wide), 0)
        chain = (lane == line + ROW * HEAD).astype(F32)
        for j in range(ROW):
            z_all[j] = cat(*split(chain), axis=1)
            p_all[j] = pack(chain[:, ROW * HEAD : (ROW + 1) * HEAD])
            chain = chain_step(g_row[j], chain) + (lane == line + j * HEAD).astype(F32)
        z_chain[...] = chain

    def send_g_col():
        total = pack(z_chain[...][:, ROW * HEAD : (ROW + 1) * HEAD])
        g_col[y] = total
        for d in FAR_FIRST:
            n = next(counter)
            conditional.append(
                [d, False, pltpu.make_async_remote_copy(
                    src_ref=g_col.at[y], dst_ref=g_col.at[y], send_sem=send.at[n], recv_sem=recv.at[n],
                    device_id=chip((y + d) % NY, x), device_id_type=MESH,
                )]
            )

            @pl.when(y + d < NY)
            def _(copy=conditional[-1][2]):
                copy.start()

    def column_chain():
        arrived_from_below(NY - 1)
        lane, line = iota((HEAD, NY * HEAD), 1), iota((HEAD, NY * HEAD), 0)
        chain = jnp.zeros((HEAD, NY * HEAD), F32)
        for q in range(NY - 1):
            longer = chain_step(g_col[q], chain) + (lane == line + q * HEAD).astype(F32)
            chain = jnp.where(q < y, longer, chain)
        z_row[...] = cat(*split(chain), axis=0)

    stages = prepare(
        r_ref, k_ref, a_ref, decay_ref, bonus_ref, y_ref, q_ref, h_ref, g_ref, coef_ref
    )

    def compute(steps=1):
        for _ in range(steps):
            next(stages, None)

    prev = copy_to(x_hbm.at[pl.ds(TOKENS - 16, 16)], prev_buf, at_seq((s + 1) % count))
    a_in = [copy_to(own_a, wa.at[0, x], chip(y, (x + d) % NX)) for d in (2, 1, 3)]
    send_yb(1)
    send_xb(0, 1)
    for load in loads:
        load.wait()

    arrived(prev)
    own = x_ref[...].astype(F32)
    before = jnp.where(s == 0, 0.0, prev_buf[...].astype(F32)[15:16, :])
    shifted = jnp.where(iota((TOKENS, WIDTH), 0) == 0, before, pltpu.roll(own, 1, 0))
    mixed = own + (shifted - own) * blend_ref[...]
    even = cat(*[mixed[:, 128 * q : 128 * q + 64] for q in range(4)], axis=1).astype(BF16)
    odd = cat(*[mixed[:, 128 * q + 64 : 128 * q + 128] for q in range(4)], axis=1).astype(BF16)
    is_even = core == 0
    xg[z, core] = jnp.where(is_even, even, odd)
    x_send[...] = jnp.where(is_even, odd, even)
    mate_x = copy_to(x_send, xg.at[z, core], mate)
    send_zx(1, 0)
    for entry in a_in:
        arrived(entry)
    send_ya(1, 0)
    send_ya(1, 1)
    arrived(mate_x)
    send_zx(1, 1)
    send_yb(2)
    send_xb(1, 2)
    compute(8)
    send_zx(2, 0)
    send_ya(2, 0)
    send_zx(2, 1)
    send_ya(2, 1)
    send_yb(3)
    send_xb(3, 2)
    compute(4)
    g_in = []
    for d in FAR_FIRST:
        to = (place + d) % ROW
        g_in.append(copy_to(g_ref.at[to], g_row.at[place], at_seq(y * ROW + to)))
    g_row[place] = g_ref[place]
    send_zx(3, 0)
    send_ya(3, 0)
    send_zx(3, 1)
    send_ya(3, 1)
    for side, step in ((1, 3), (-1, 3), (1, 4)):
        arrived(yb[side, step])
    send_xb(5, 3)
    compute(100)
    row_chain()
    send_g_col()
    for entry in list(zx.values()) + list(ya.values()):
        arrived(entry)

    partial = []
    for half, weights in enumerate((wa, wb)):
        if half:
            for entry in waiting[:-1]:
                arrived(entry)
        total = jnp.zeros((2 * TOKENS, 256), F32)
        for slot, offset in enumerate(OFFSETS):
            total = total + dot(
                xg[row_at(offset)].reshape(2 * TOKENS, 256), weights[slot].reshape(256, 256)
            )
        p_send[half] = total.reshape(2, TOKENS, 256)
        partial.append(copy_to(p_send.at[half, 1 - core], p_recv.at[half], mate))
    values, doubled = [], []
    for half in range(2):
        arrived(partial[half])
        values.append((p_send[half, core] + p_recv[half]).astype(BF16))
        for h in range(HEADS // 2 * half, HEADS // 2 * (half + 1)):
            v = values[half][:, HEAD * (h % 4) : HEAD * (h % 4 + 1)]
            doubled.append(cat(v, v, axis=0))
            l_send[h] = pack(dot(h_ref[h], doubled[h]))
    value = cat(*values, axis=1)
    l_in = []
    for d in FAR_FIRST:
        to = (place + d) % ROW
        l_in.append(copy_to(l_send.at[to], l_row.at[place], at_seq(y * ROW + to)))
    l_row[place] = l_send[place]
    column_chain()
    chain = z_chain[...][:, : ROW * HEAD]
    row_total = cat(*split(chain), axis=0)
    for entry in l_in:
        arrived(entry)
    lows = l_row[...].reshape(ROW * HEAD, 2 * HEAD)
    total = fold(dot(row_total, lows))
    t_send[...] = pack(total[:HEAD] + total[HEAD:])
    for d in FAR_FIRST:
        n = next(counter)
        conditional.append(
            [d, False, pltpu.make_async_remote_copy(
                src_ref=t_send, dst_ref=t_col.at[y], send_sem=send.at[n], recv_sem=recv.at[n],
                device_id=chip((y + d) % NY, x), device_id_type=MESH,
            )]
        )

        @pl.when(y + d < NY)
        def _(copy=conditional[-1][2]):
            copy.start()

    wide = ROW * HEAD
    span = z_all.shape[2] // 2
    from_row = []
    for j in range(ROW):
        both = cat(z_all[j, :, :wide], z_all[j, :, span : span + wide], axis=1)
        from_row.append(dot(both, cat(lows, lows, axis=0)))
    reads = [dot(y_ref[h], doubled[h]) for h in range(HEADS)]
    extra = coef_ref[...] * value.astype(F32)
    gate = gate_ref[...].astype(F32)

    arrived_from_below()
    entering = fold(dot(z_row[...], t_col[...].reshape(NY * HEAD, 2 * HEAD)))
    entering = pack(entering[:HEAD] + entering[HEAD:])
    twice = cat(entering, entering, axis=0)
    entered = dot(p_all[...].reshape(ROW * HEAD, 2 * HEAD), twice)
    for j in range(ROW):
        s_send[j] = pack(fold(from_row[j] + entered[HEAD * j : HEAD * (j + 1)]))
    s_wait = []
    for d in FAR_FIRST:
        to = (place + d) % ROW
        s_wait.append(copy_to(s_send.at[to], s_in.at[place], at_seq(y * ROW + to)))
    s_in[place] = s_send[place]
    for entry in s_wait:
        arrived(entry)
    for h in range(HEADS):
        state = s_in[h]
        reads[h] = reads[h] + fold(dot(q_ref[h], cat(state, state, axis=0)))
    read = cat(*reads, axis=1)
    centre = read - head_sums(read) * (1.0 / HEAD)
    spread = head_sums(centre * centre) * (1.0 / HEAD)
    normed = centre * lax.rsqrt(spread + NORM_EPS) * scale_ref[...] + offset_ref[...]
    out_ref[...] = ((normed + extra) * gate).astype(BF16)

    finish()


COPIES = 128
SCRATCH = (
    pltpu.VMEM((TOKENS, WIDTH), BF16),
    pltpu.VMEM((TOKENS, WIDTH), BF16),
    pltpu.VMEM((TOKENS, WIDTH), BF16),
    pltpu.VMEM((TOKENS, WIDTH), BF16),
    pltpu.VMEM((TOKENS, WIDTH), F32),
    pltpu.VMEM((TOKENS, WIDTH), BF16),
    pltpu.VMEM((HEADS, TOKENS, 2 * TOKENS), BF16),
    pltpu.VMEM((HEADS, TOKENS, 2 * HEAD), BF16),
    pltpu.VMEM((HEADS, HEAD, 2 * TOKENS), BF16),
    pltpu.VMEM((HEADS, HEAD, 2 * HEAD), BF16),
    pltpu.VMEM((TOKENS, WIDTH), F32),
    pltpu.VMEM((16, WIDTH), BF16),
    pltpu.VMEM((TOKENS, 256), BF16),
    pltpu.VMEM((NZ, 2, TOKENS, 256), BF16),
    pltpu.VMEM((NY, NX, HEAD, 256), BF16),
    pltpu.VMEM((NY, NX, HEAD, 256), BF16),
    pltpu.VMEM((2, 2, TOKENS, 256), F32),
    pltpu.VMEM((2, TOKENS, 256), F32),
    pltpu.VMEM((ROW, HEAD, 2 * HEAD), BF16),
    pltpu.VMEM((NY, HEAD, 2 * HEAD), BF16),
    pltpu.VMEM((HEAD, 640), F32),
    pltpu.VMEM((ROW, HEAD, 2 * 640), BF16),
    pltpu.VMEM((ROW, HEAD, 2 * HEAD), BF16),
    pltpu.VMEM((2 * HEAD, NY * HEAD), BF16),
    pltpu.VMEM((HEADS, HEAD, 2 * HEAD), BF16),
    pltpu.VMEM((ROW, HEAD, 2 * HEAD), BF16),
    pltpu.VMEM((HEAD, 2 * HEAD), BF16),
    pltpu.VMEM((NY, HEAD, 2 * HEAD), BF16),
    pltpu.VMEM((ROW, HEAD, 2 * HEAD), BF16),
    pltpu.VMEM((HEADS, HEAD, 2 * HEAD), BF16),
    pltpu.SemaphoreType.DMA((COPIES,)),
    pltpu.SemaphoreType.DMA((COPIES,)),
    pltpu.SemaphoreType.DMA((8,)),
)


def shards(
    activation_entries,
    content_mapping_matrix,
    content_lagged_blend,
    acceptance_vectors,
    address_vectors_given,
    inline_adaptation_speed,
    memory_fading_factors,
    result_filter_given,
    extra_coordinate_factors,
    group_layernorm_scaling,
    group_layernorm_offset,
):
    vmem = pl.BlockSpec(memory_space=pltpu.VMEM)

    def row(vector):
        return vector.reshape(1, WIDTH)

    hbm = pl.BlockSpec(memory_space=pltpu.HBM)

    def pin(array):
        return pltpu.with_memory_space_constraint(array, pltpu.HBM)

    return pl.pallas_call(
        time_mix,
        out_shape=jax.ShapeDtypeStruct((TOKENS, WIDTH), BF16),
        in_specs=[hbm] * 7 + [vmem] * 4,
        out_specs=vmem,
        scratch_shapes=SCRATCH,
        compiler_params=pltpu.CompilerParams(
            collective_id=0, has_side_effects=True, vmem_limit_bytes=48 << 20
        ),
        name="time_mix",
    )(
        pin(activation_entries),
        pin(content_mapping_matrix),
        pin(acceptance_vectors),
        pin(address_vectors_given),
        pin(inline_adaptation_speed),
        pin(memory_fading_factors),
        pin(result_filter_given),
        pin(row(content_lagged_blend)),
        pin(row(extra_coordinate_factors)),
        pin(row(group_layernorm_scaling)),
        pin(row(group_layernorm_offset)),
    )


def solution(mesh):
    return jax.shard_map(
        shards,
        mesh=mesh,
        in_specs=(
            P("seq", "fsdp"),
            P("seq", "fsdp"),
            P("fsdp"),
            P("seq", "fsdp"),
            P("seq", "fsdp"),
            P("seq", "fsdp"),
            P("seq", "fsdp"),
            P("seq", "fsdp"),
            P("fsdp"),
            P("fsdp"),
            P("fsdp"),
        ),
        out_specs=P("seq", "fsdp"),
        check_vma=False,
    )
```
